32 devices in a mesh: harm: 16 (over z, x, core), bus: 2 (over y).
Axes of the slice: x: 2, y: 2, z: 4, core: 2. Of those that a mesh axis runs over, the one named last changes fastest.
Arguments:
- conv_volt: bfloat16 [2, 64, 128, 128], P(None, None, ('bus', 'harm')), may hold values from -0.75 to 0.75
- conv_power: float32 [128, 128], P(('bus', 'harm')), may hold values from 0.2 to 2
- conv_type: int32 [128], P(('bus', 'harm')), may hold values from 0 to 7
- type_steep: float32 [8], replicated, may hold values from 0.5 to 4
- conv_bus: int32 [128], P(('bus', 'harm')), may hold values from 0 to 511, as said below
- admittance: float32 [2, 4, 64, 512], P(None, None, 'harm', 'bus'), may hold values from -0.5 to 1
- link_offset: int32 [3, 512], P(None, 'bus'), may hold values from -8 to 8, as said below
Outputs:
- bus_volt: bfloat16 [2, 64, 512, 128], P(None, 'harm', 'bus')
- conv_next: bfloat16 [2, 64, 128, 128], P(None, None, ('bus', 'harm'))
The draws below stay inside these ranges and needn't reach their ends.
Inputs may be any that keep to these rules, and one draw needn't show every extreme that they name: `conv_bus`: converter c is attached to one of the buses from (c // 4) * 16 to (c // 4 + 1) * 16 - 1; a bus may carry several converters. `link_offset`: the first line of every bus spans exactly 8 buses, up or down; the others span 1 to 8 buses; no offset is zero.
All inputs are finite; a program needn't handle non-finite values.
Results may differ from the reference program's by a relative error of at most 0.0057.
Values may be sent and summed in bfloat16 or wider, within the bound.
A program may use at most 64 MiB of HBM per device.

```python
import math
import jax
import jax.numpy as jnp
from jax import lax

H = 64
NT = 1024
S = 128
CONV_DEV = 4
BUS_SUB = 16
TYPES = 8
LINKS = 3
REACH = 8
ITERS = 3
CONVS = 128
BUSES = 512


def draw_conv_bus(key, part):
    keys = jax.random.split(jax.random.fold_in(key, 11), 3)
    first_pick = jax.random.randint(keys[0], (CONVS,), 0, BUS_SUB)
    second_pick = jax.random.randint(keys[1], (CONVS,), 0, BUS_SUB)
    rotation = jax.random.randint(keys[2], (CONVS // CONV_DEV,), 0, BUS_SUB)
    group_num = jnp.arange(CONVS, dtype=jnp.int32) // CONV_DEV
    local_bus = (jnp.minimum(first_pick, second_pick) + rotation[group_num]) % BUS_SUB
    return (group_num * BUS_SUB + local_bus).astype(jnp.int32)


def draw_link_offset(key, part):
    keys = jax.random.split(jax.random.fold_in(key, 23), 2)
    distance = jax.random.randint(keys[0], (LINKS, BUSES), 1, REACH + 1)
    distance = jnp.where(jnp.arange(LINKS, dtype=jnp.int32)[:, None] == 0, REACH, distance)
    direction = jax.random.randint(keys[1], (LINKS, BUSES), 0, 2) * 2 - 1
    return (distance * direction).astype(jnp.int32)


def draw_admittance(key, part):
    keys = jax.random.split(jax.random.fold_in(key, 37), 3)
    inverse_real = jax.random.uniform(keys[0], (H, BUSES), jnp.float32, 0.4, 1.0)
    inverse_imag = jnp.clip(0.15 * jax.random.normal(keys[1], (H, BUSES), jnp.float32), -0.45, 0.45)
    lines = jnp.clip(0.17 * jax.random.normal(keys[2], (2, LINKS, H, BUSES), jnp.float32), -0.5, 0.5)
    inverse = jnp.stack([inverse_real, inverse_imag])[:, None]
    return jnp.concatenate([inverse, lines], axis=1).astype(jnp.float32)


def place_ends(array, rng, least, largest):
    shape = array.shape
    index_at = [jax.random.randint(jax.random.fold_in(rng, axis), (), 0, shape[axis]) for axis in range(len(shape))]
    array = array.at[tuple(index_at)].set(least)
    longest = shape.index(max(shape))
    index_at[longest] = (index_at[longest] + 1) % shape[longest]
    return array.at[tuple(index_at)].set(largest)


def levels(key, extent, pieces, least, high):
    def one(position, shards_of):
        heights = jax.random.uniform(jax.random.fold_in(jax.random.fold_in(key, 6), position), (shards_of,), jnp.float32, least / len(pieces), high / len(pieces))
        return jnp.repeat(jnp.exp(heights), extent[position] // shards_of).reshape((-1,) + (1,) * (len(extent) - position - 1))

    level = one(*pieces[0])
    for cut in pieces[1:]:
        level = level * one(*cut)
    return level


def centred(key, dims, scale, most, pieces=(), kind=jnp.bfloat16):
    drawn = scale * jax.random.normal(key, dims, jnp.float32)
    if pieces:
        drawn = drawn * levels(key, dims, pieces, -0.22, 0.18)
    return jnp.clip(drawn, -most, most).astype(kind)


def setup_inputs(seed: int = 0) -> dict:
    arg_keys = jax.random.split(jax.random.key(seed), 8)
    conv_volt = centred(arg_keys[0], (2, H, CONVS, S), 0.125, 0.75, ((2, 32),))
    conv_power = jnp.clip(jnp.exp(math.log(2.0) - 2.3025851 * jax.random.uniform(arg_keys[1], (CONVS, S), jnp.float32) ** levels(arg_keys[1], (CONVS, S), ((0, 32),), -0.2, 0.2)), 0.2, 2.0)
    conv_type = place_ends(jax.random.randint(arg_keys[2], (CONVS,), 0, TYPES), jax.random.fold_in(arg_keys[2], 1), 0, TYPES - 1).astype(jnp.int32)
    type_steep = jnp.clip(jax.random.uniform(arg_keys[3], (TYPES,), jnp.float32, 0.5, 4.0), 0.5, 4.0)
    conv_bus = draw_conv_bus(jax.random.fold_in(arg_keys[7], 71), 0)
    admittance = draw_admittance(jax.random.fold_in(arg_keys[7], 71), 0)
    link_offset = draw_link_offset(jax.random.fold_in(arg_keys[7], 71), 0)
    return {"conv_volt": conv_volt, "conv_power": conv_power, "conv_type": conv_type, "type_steep": type_steep, "conv_bus": conv_bus, "admittance": admittance, "link_offset": link_offset}


def make_basis():
    orders = jnp.arange(1, H + 1, dtype=jnp.int32)
    samples = jnp.arange(NT, dtype=jnp.int32)
    phases = ((orders[:, None] * samples[None, :]) % NT).astype(jnp.float32) * (2.0 * math.pi / NT)
    return jnp.concatenate([jnp.cos(phases), -jnp.sin(phases)], axis=0).astype(jnp.bfloat16)


def complex_product(left_real, left_imag, right_real, right_imag):
    return left_real * right_real - left_imag * right_imag, left_real * right_imag + left_imag * right_real


def reference(conv_volt, conv_power, conv_type, type_steep, conv_bus, admittance, link_offset):
    harmonic_basis = make_basis().astype(jnp.float32)
    steepness = type_steep[conv_type]
    volt_rows = conv_volt.reshape(2 * H, CONVS, S)

    def evaluate(group_num):
        first_row = (group_num * CONV_DEV).astype(jnp.int32)
        volt_group = lax.dynamic_slice_in_dim(volt_rows, first_row, CONV_DEV, 1).astype(jnp.float32)
        power_group = lax.dynamic_slice_in_dim(conv_power, first_row, CONV_DEV, 0)
        steep_group = lax.dynamic_slice_in_dim(steepness, first_row, CONV_DEV, 0)
        waveform = jnp.einsum("kcs,kn->csn", volt_group, harmonic_basis)
        current = (power_group[:, :, None] * jnp.tanh(steep_group[:, None, None] * waveform)).astype(jnp.bfloat16)
        spectra = jnp.einsum("csn,kn->kcs", current.astype(jnp.float32), harmonic_basis) * (NT ** -0.5)
        return spectra.astype(jnp.bfloat16)

    groups = lax.map(evaluate, jnp.arange(CONVS // CONV_DEV, dtype=jnp.int32))
    spectra = jnp.transpose(groups, (1, 0, 2, 3)).reshape(2, H, CONVS, S)
    bus_numbers = jnp.arange(BUSES, dtype=jnp.int32)

    def solve(harmonic):
        spectra_here = spectra[:, harmonic].astype(jnp.float32)
        summed = jnp.zeros((2, BUSES, S), jnp.float32).at[:, conv_bus, :].add(spectra_here)
        rounded = lax.optimization_barrier(summed.astype(jnp.bfloat16))
        inject_real = rounded[0].astype(jnp.float32)
        inject_imag = rounded[1].astype(jnp.float32)
        coeffs = admittance[:, :, harmonic]
        diag_real = coeffs[0, 0][:, None]
        diag_imag = coeffs[1, 0][:, None]
        volt_real, volt_imag = complex_product(diag_real, diag_imag, inject_real, inject_imag)
        for sweep_index in range(ITERS - 1):
            total_real, total_imag = inject_real, inject_imag
            for line_num in range(LINKS):
                target = bus_numbers + link_offset[line_num]
                inside = ((target >= 0) & (target < BUSES))[:, None]
                clipped = jnp.clip(target, 0, BUSES - 1)
                near_real = jnp.where(inside, volt_real[clipped], 0.0)
                near_imag = jnp.where(inside, volt_imag[clipped], 0.0)
                term_real, term_imag = complex_product(coeffs[0, 1 + line_num][:, None], coeffs[1, 1 + line_num][:, None], near_real, near_imag)
                total_real = total_real + term_real
                total_imag = total_imag + term_imag
            volt_real, volt_imag = complex_product(diag_real, diag_imag, total_real, total_imag)
        bus_here = jnp.stack([volt_real, volt_imag]).astype(jnp.bfloat16)
        return bus_here, bus_here[:, conv_bus, :]

    bus_all, conv_all = lax.map(solve, jnp.arange(H, dtype=jnp.int32))
    return jnp.transpose(bus_all, (1, 0, 2, 3)), jnp.transpose(conv_all, (1, 0, 2, 3))
```

```python
import functools
import math

import jax
import jax.numpy as jnp
import numpy as np
from jax import lax
from jax.experimental import pallas as pl
from jax.experimental.pallas import tpu as pltpu
from jax.sharding import PartitionSpec as P

NT = 1024
LANES = 128
CHUNKS = 4


def make_basis(orders):
    samples = np.arange(NT)
    phases = (np.arange(1, orders + 1)[:, None] * samples[None, :] % NT) * (2.0 * math.pi / NT)
    return np.concatenate([np.cos(phases), -np.sin(phases)], axis=0).astype(np.float32)


def kernel(
    nh,
    ny,
    volt_hbm,
    power_hbm,
    type_ref,
    steep_ref,
    bus_ref,
    adm_hbm,
    off_hbm,
    fwd_hbm,
    inv_hbm,
    out_ref,
    next_ref,
    volt_ref,
    power_ref,
    adm_ref,
    off_ref,
    fwd_ref,
    inv_ref,
    wide,
    volts,
    send,
    recv,
    my_bus,
    buses,
    adm_side,
    off_side,
    weights,
    resp,
    send_back,
    load_sem,
    send_sem,
    recv_sem,
):
    me = lax.axis_index("harm")
    y = lax.axis_index("bus")
    hl = adm_ref.shape[2]
    block = adm_ref.shape[3]
    links = off_ref.shape[0]
    conv = power_ref.shape[0]
    sub = block // nh
    tiles = block // LANES
    around = LANES // sub
    rows = 8 * (around + 2)
    has_left = y > 0
    has_right = y < ny - 1
    send_right = jnp.logical_and(has_right, me == nh - 1)
    send_left = jnp.logical_and(has_left, me == 0)

    pairs = (
        (volt_hbm, volt_ref),
        (fwd_hbm, fwd_ref),
        (power_hbm, power_ref),
        (inv_hbm, inv_ref),
        (adm_hbm, adm_ref),
        (off_hbm, off_ref),
    )
    loads = [pltpu.make_async_copy(src, dst, load_sem.at[i]) for i, (src, dst) in enumerate(pairs)]
    for load in loads:
        load.start()

    barrier = pltpu.get_barrier_semaphore()

    def greet(d, by):
        pl.semaphore_signal(barrier, inc=1, device_id={"harm": d, "bus": by})

    def each(low, body):
        def step(i, carry):
            body(i)
            return carry

        lax.fori_loop(low, nh, step, 0)

    def peer(s):
        return lax.rem(me + s, nh)

    each(1, lambda s: greet(peer(s), y))

    @pl.when(has_left)
    def _():
        each(0, lambda d: greet(d, y - 1))

    @pl.when(has_right)
    def _():
        each(0, lambda d: greet(d, y + 1))

    @pl.when(jnp.logical_not(has_left))
    def _():
        recv[0] = jnp.zeros(recv.shape[1:], recv.dtype)
        buses[0] = jnp.zeros(buses.shape[1:], buses.dtype)
        adm_side[0] = jnp.zeros(adm_side.shape[1:], adm_side.dtype)
        off_side[0] = jnp.zeros(off_side.shape[1:], off_side.dtype)

    @pl.when(jnp.logical_not(has_right))
    def _():
        recv[nh + 1] = jnp.zeros(recv.shape[1:], recv.dtype)
        buses[nh + 1] = jnp.zeros(buses.shape[1:], buses.dtype)
        adm_side[1] = jnp.zeros(adm_side.shape[1:], adm_side.dtype)
        off_side[1] = jnp.zeros(off_side.shape[1:], off_side.dtype)

    for load in loads[:4]:
        load.wait()
    span = volt_ref.shape[0] // conv
    wide[0 : span * conv] = volt_ref[...].astype(jnp.float32)
    for c in range(conv):
        volts[:, LANES * c : LANES * (c + 1)] = wide[pl.ds(c, span, stride=conv), :].astype(jnp.bfloat16)

    def steepness(c):
        value = steep_ref[0]
        for kind in range(1, steep_ref.shape[0]):
            value = jnp.where(type_ref[c] == kind, steep_ref[kind], value)
        return jnp.full((1, LANES), value, jnp.float32)

    steep = jnp.concatenate([steepness(c) for c in range(conv)], axis=1)
    power = jnp.concatenate([power_ref[c : c + 1, :] for c in range(conv)], axis=1) * NT ** (-0.5)
    part = NT // CHUNKS
    spectra = jnp.zeros((span, conv * LANES), jnp.float32)
    for q in range(CHUNKS):
        wave = jnp.dot(fwd_ref[part * q : part * (q + 1), :], volts[...], preferred_element_type=jnp.float32)
        now = jnp.tanh(steep * wave).astype(jnp.bfloat16)
        spectra = spectra + jnp.dot(
            inv_ref[:, part * q : part * (q + 1)], now, preferred_element_type=jnp.float32
        )
    spectra = spectra * power
    for c in range(conv):
        wide[pl.ds(c, span, stride=conv), :] = spectra[:, LANES * c : LANES * (c + 1)]
    send[...] = wide[0 : span * conv].reshape(nh, hl, 8, LANES).astype(jnp.bfloat16)

    for load in loads[4:]:
        load.wait()
    first = (y * nh + me) * sub
    row8 = lax.broadcasted_iota(jnp.int32, (8, LANES), 0) % conv
    numbers = jnp.zeros((8, LANES), jnp.float32)
    for c in range(conv):
        numbers = jnp.where(row8 == c, (bus_ref[c] - first).astype(jnp.float32), numbers)
    my_bus[...] = numbers.astype(jnp.bfloat16)

    pl.semaphore_wait(barrier, nh - 1 + nh * has_left.astype(jnp.int32) + nh * has_right.astype(jnp.int32))

    def remote(src, dst, out, into, d, by):
        return pltpu.make_async_remote_copy(
            src_ref=src,
            dst_ref=dst,
            send_sem=send_sem.at[out],
            recv_sem=recv_sem.at[into],
            device_id={"harm": d, "bus": by},
        )

    def bus_copy(d, slot, by, out, into):
        return remote(my_bus, buses.at[slot], out, into, d, by)

    def spec_copy(d, slot, by, out, into):
        return remote(send.at[d], recv.at[slot], out, into, d, by)

    def ret_copy(d, source):
        place = next_ref.at[:, pl.ds(source * hl, hl)]
        return remote(send_back.at[d], place, 6, 6, d, y)

    def side_copies(side):
        by = y + 1 if side == 0 else y - 1
        start = block - LANES if side == 0 else 0
        return (
            remote(adm_ref.at[:, :, :, pl.ds(start, LANES)], adm_side.at[side], 7 + side, 7 + side, me, by),
            remote(off_ref.at[:, pl.ds(start, LANES)], off_side.at[side], 9 + side, 9 + side, me, by),
        )

    each(1, lambda s: bus_copy(peer(s), me + 1, y, 0, 0).start())
    each(1, lambda s: spec_copy(peer(s), me + 1, y, 3, 3).start())

    @pl.when(send_right)
    def _():
        each(0, lambda d: bus_copy(d, 0, y + 1, 1, 1).start())
        each(0, lambda d: spec_copy(d, 0, y + 1, 4, 4).start())

    @pl.when(send_left)
    def _():
        each(0, lambda d: bus_copy(d, nh + 1, y - 1, 2, 2).start())
        each(0, lambda d: spec_copy(d, nh + 1, y - 1, 5, 5).start())

    @pl.when(has_right)
    def _():
        for copy in side_copies(0):
            copy.start()

    @pl.when(has_left)
    def _():
        for copy in side_copies(1):
            copy.start()

    recv[me + 1] = send[me]
    buses[me + 1] = my_bus[...]

    lane = lax.broadcasted_iota(jnp.int32, (1, LANES), 1)
    is_right = lane < LANES // 2

    def adm_row(p, k, h, t, beyond):
        def row_of(t):
            if t < 0:
                return adm_side[0, p, k, h : h + 1, :]
            if t >= tiles:
                return adm_side[1, p, k, h : h + 1, :]
            return adm_ref[p, k, h : h + 1, LANES * t : LANES * (t + 1)]

        return jnp.where(is_right, row_of(t + 1), row_of(t - 1)) if beyond else row_of(t)

    def off_row(k, t, beyond):
        def row_of(t):
            if t < 0:
                return off_side[0, k : k + 1, :]
            if t >= tiles:
                return off_side[1, k : k + 1, :]
            return off_ref[k : k + 1, LANES * t : LANES * (t + 1)]

        return jnp.where(is_right, row_of(t + 1), row_of(t - 1)) if beyond else row_of(t)

    def fill(t, beyond, low, high):
        band = lax.broadcasted_iota(jnp.int32, (high - low, LANES), 0) + low
        shift = LANES if beyond else 0
        masks = [
            band == jnp.bitwise_and(lane + shift + off_row(k, t, beyond), 2 * LANES - 1) for k in range(links)
        ]
        at = 2 * shift
        for h in range(hl):
            d_real, d_imag = adm_row(0, 0, h, t, beyond), adm_row(1, 0, h, t, beyond)
            total_real = jnp.zeros(band.shape, jnp.float32)
            total_imag = jnp.zeros(band.shape, jnp.float32)
            for k in range(links):
                l_real, l_imag = adm_row(0, 1 + k, h, t, beyond), adm_row(1, 1 + k, h, t, beyond)
                total_real += jnp.where(masks[k], d_real * l_real - d_imag * l_imag, 0.0)
                total_imag += jnp.where(masks[k], d_real * l_imag + d_imag * l_real, 0.0)
            weights[h, t, low:high, at : at + LANES] = total_real.astype(jnp.bfloat16)
            weights[h, t, low:high, at + LANES : at + 2 * LANES] = total_imag.astype(jnp.bfloat16)

    for t in range(tiles):
        fill(t, False, 0, LANES + 16)
        fill(t, False, 2 * LANES - 16, 2 * LANES)
        for h in range(hl):
            weights[h, t, LANES + 16 : 2 * LANES - 16, :] = jnp.zeros((LANES - 32, 4 * LANES), jnp.bfloat16)
            weights[h, t, 16 : LANES - 16, 2 * LANES :] = jnp.zeros((LANES - 32, 2 * LANES), jnp.bfloat16)

    @pl.when(has_left)
    def _():
        for copy in side_copies(0):
            copy.wait_recv()

    @pl.when(has_right)
    def _():
        for copy in side_copies(1):
            copy.wait_recv()

    for t in range(tiles):
        for low, high in ((LANES - 16, LANES + 16), (2 * LANES - 16, 2 * LANES), (0, 16)):
            fill(t, True, low, high)

    def all_of(ref, count, out, into):
        return remote(ref.at[pl.ds(0, count)], ref.at[pl.ds(0, count)], out, into, me, y)

    all_of(buses, nh - 1, 0, 0).wait_recv()

    @pl.when(has_left)
    def _():
        bus_copy(0, 0, y, 1, 1).wait_recv()

    @pl.when(has_right)
    def _():
        bus_copy(0, nh + 1, y, 2, 2).wait_recv()

    row = lax.broadcasted_iota(jnp.int32, (rows, LANES), 0)
    is_real = row % 8 < conv
    base = jnp.bitwise_and((row // 8 - 1) * sub, 2 * LANES - 1)
    own = 8 * around
    for t in range(tiles):
        near = buses[around * t : around * (t + 1) + 2].astype(jnp.float32).reshape(rows, LANES)
        at_bus = base + near.astype(jnp.int32)
        hits = [at_bus == lane, at_bus == lane + LANES]
        picked = jnp.where(hits[0], 1.0, 0.0)
        pick_real = jnp.where(is_real, picked, 0.0)[8 : 8 + own].astype(jnp.bfloat16)
        pick_imag = jnp.where(is_real, 0.0, picked)[8 : 8 + own].astype(jnp.bfloat16)
        for h in range(hl):
            start_real, start_imag = [], []
            for side in (False, True):
                d_real, d_imag = adm_row(0, 0, h, t, side), adm_row(1, 0, h, t, side)
                start_real.append(jnp.where(hits[side], jnp.where(is_real, d_real, -d_imag), 0.0))
                start_imag.append(jnp.where(hits[side], jnp.where(is_real, d_imag, d_real), 0.0))
            now_real, now_imag = start_real, start_imag
            for last in (False, True):
                state = jnp.concatenate(
                    [jnp.concatenate(now_real, axis=1), jnp.concatenate(now_imag, axis=1)], axis=0
                ).astype(jnp.bfloat16)
                width = 2 * LANES if last else 4 * LANES
                both = jnp.dot(state, weights[h, t, :, 0:width], preferred_element_type=jnp.float32)
                new_real, new_imag = [], []
                for a in range(1 if last else 2):
                    at = 2 * LANES * a
                    left, right = both[:, at : at + LANES], both[:, at + LANES : at + 2 * LANES]
                    new_real.append(start_real[a] + left[:rows] - right[rows:])
                    new_imag.append(start_imag[a] + right[:rows] + left[rows:])
                now_real, now_imag = new_real, new_imag
            real_t = now_real[0].T.astype(jnp.bfloat16)
            imag_t = now_imag[0].T.astype(jnp.bfloat16)
            resp[h, t, own : own + LANES, :] = real_t
            resp[h, t, own + LANES :, :] = imag_t
            chosen = jnp.dot(pick_real, real_t, preferred_element_type=jnp.float32)
            chosen += jnp.dot(pick_imag, imag_t, preferred_element_type=jnp.float32)
            resp[h, t, 0:own, :] = chosen.astype(jnp.bfloat16)

    all_of(recv, nh - 1, 3, 3).wait_recv()

    @pl.when(has_left)
    def _():
        spec_copy(0, 0, y, 4, 4).wait_recv()

    @pl.when(has_right)
    def _():
        spec_copy(0, nh + 1, y, 5, 5).wait_recv()

    arrived = []
    for t in range(tiles):
        for h in range(hl):
            here = recv[around * t : around * (t + 1) + 2, h].astype(jnp.float32)
            arrived.append(here.reshape(rows, LANES).astype(jnp.bfloat16))
            at_conv = jnp.dot(resp[h, t, 0:own, :], arrived[-1], preferred_element_type=jnp.float32)
            at_conv = at_conv.reshape(around, 2, conv, LANES).astype(jnp.bfloat16)
            send_back[around * t : around * (t + 1), :, h] = at_conv
    each(1, lambda s: ret_copy(peer(s), me).start())
    next_ref[:, pl.ds(me * hl, hl)] = send_back[me]
    for t in range(tiles):
        for h in range(hl):
            solved = jnp.dot(resp[h, t, own:, :], arrived[t * hl + h], preferred_element_type=jnp.float32)
            out_ref[:, h, LANES * t : LANES * (t + 1)] = solved.astype(jnp.bfloat16).reshape(2, LANES, LANES)

    all_of(buses, nh - 1, 0, 0).wait_send()
    all_of(recv, nh - 1, 3, 3).wait_send()

    @pl.when(has_right)
    def _():
        for copy in side_copies(0):
            copy.wait_send()

    @pl.when(has_left)
    def _():
        for copy in side_copies(1):
            copy.wait_send()

    @pl.when(send_right)
    def _():
        all_of(buses, nh, 1, 1).wait_send()
        all_of(recv, nh, 4, 4).wait_send()

    @pl.when(send_left)
    def _():
        all_of(buses, nh, 2, 2).wait_send()
        all_of(recv, nh, 5, 5).wait_send()

    all_of(send_back, nh - 1, 6, 6).wait_send()
    all_of(send_back, nh - 1, 6, 6).wait_recv()


def store(volt_ref, next_ref, volt_out, next_out, sems):
    copies = [pltpu.make_async_copy(volt_ref.at[p], volt_out.at[p], sems.at[p]) for p in range(2)]
    copies.append(pltpu.make_async_copy(next_ref, next_out, sems.at[2]))
    for copy in copies:
        copy.start()
    for copy in copies:
        copy.wait()


def local(nh, ny, conv_volt, conv_power, conv_type, type_steep, conv_bus, admittance, link_offset):
    _, orders, conv, snaps = conv_volt.shape
    hl = orders // nh
    block = admittance.shape[3]
    tiles = block // LANES
    around = LANES * nh // block
    rows = 8 * (around + 2)
    span = 2 * orders
    basis = make_basis(orders)
    regrouped = basis.reshape(2, orders, NT).transpose(1, 0, 2).reshape(span, NT)
    vmem = pl.BlockSpec(memory_space=pltpu.VMEM)
    smem = pl.BlockSpec(memory_space=pltpu.SMEM)
    anywhere = pl.BlockSpec(memory_space=pl.ANY)
    bf16 = jnp.bfloat16
    dma = pltpu.SemaphoreType.DMA
    volt_shape, next_shape = (2, hl, block, snaps), (2, orders, conv, snaps)
    solved = pl.pallas_call(
        functools.partial(kernel, nh, ny),
        out_shape=(pltpu.VMEM(volt_shape, bf16), pltpu.VMEM(next_shape, bf16)),
        in_specs=[anywhere, anywhere, smem, smem, smem, anywhere, anywhere, anywhere, anywhere],
        out_specs=(vmem, vmem),
        scratch_shapes=[
            pltpu.VMEM((span * conv, snaps), bf16),
            pltpu.VMEM((conv, snaps), jnp.float32),
            pltpu.VMEM(admittance.shape, jnp.float32),
            pltpu.VMEM(link_offset.shape, jnp.int32),
            pltpu.VMEM((NT, span), bf16),
            pltpu.VMEM((span, NT), bf16),
            pltpu.VMEM((span * conv + 8, LANES), jnp.float32),
            pltpu.VMEM((span, conv * LANES), bf16),
            pltpu.VMEM((nh, hl, 8, LANES), bf16),
            pltpu.VMEM((nh + 2, hl, 8, LANES), bf16),
            pltpu.VMEM((8, LANES), bf16),
            pltpu.VMEM((nh + 2, 8, LANES), bf16),
            pltpu.VMEM((2,) + admittance.shape[:3] + (LANES,), jnp.float32),
            pltpu.VMEM((2, link_offset.shape[0], LANES), jnp.int32),
            pltpu.VMEM((hl, tiles, 2 * LANES, 4 * LANES), bf16),
            pltpu.VMEM((hl, tiles, 8 * around + 2 * LANES, rows), bf16),
            pltpu.VMEM((nh, 2, hl, conv, LANES), bf16),
            dma((6,)),
            dma((11,)),
            dma((11,)),
        ],
        compiler_params=pltpu.CompilerParams(collective_id=0, has_side_effects=True, vmem_limit_bytes=56 * 2**20),
        name="power_flow",
    )(
        conv_volt.reshape(span * conv, snaps),
        conv_power,
        conv_type,
        type_steep,
        conv_bus,
        admittance,
        link_offset,
        jnp.asarray(basis.T, bf16),
        jnp.asarray(regrouped, bf16),
    )
    return pl.pallas_call(
        store,
        out_shape=(jax.ShapeDtypeStruct(volt_shape, bf16), jax.ShapeDtypeStruct(next_shape, bf16)),
        in_specs=[vmem, vmem],
        out_specs=(anywhere, anywhere),
        scratch_shapes=[dma((3,))],
        compiler_params=pltpu.CompilerParams(vmem_limit_bytes=32 * 2**20),
        name="store_results",
    )(*solved)


def solution(mesh):
    in_specs = (
        P(None, None, ("bus", "harm"), None),
        P(("bus", "harm"), None),
        P(("bus", "harm")),
        P(),
        P(("bus", "harm")),
        P(None, None, "harm", "bus"),
        P(None, "bus"),
    )
    out_specs = (P(None, "harm", "bus", None), P(None, None, ("bus", "harm"), None))
    body = functools.partial(local, mesh.shape["harm"], mesh.shape["bus"])
    return jax.shard_map(body, mesh=mesh, in_specs=in_specs, out_specs=out_specs, check_vma=False)
```

```python
import functools
import math

import jax
import jax.numpy as jnp
import numpy as np
from jax import lax
from jax.experimental import pallas as pl
from jax.experimental.pallas import tpu as pltpu
from jax.sharding import PartitionSpec as P

NT = 1024
LANES = 128
CHUNKS = 4


def make_basis(orders):
    samples = np.arange(NT)
    phases = (np.arange(1, orders + 1)[:, None] * samples[None, :] % NT) * (2.0 * math.pi / NT)
    return np.concatenate([np.cos(phases), -np.sin(phases)], axis=0).astype(np.float32)


def kernel(
    nh,
    ny,
    volt_hbm,
    power_hbm,
    type_hbm,
    steep_hbm,
    bus_hbm,
    adm_hbm,
    off_hbm,
    fwd_hbm,
    inv_hbm,
    out_ref,
    next_ref,
    volt_ref,
    type_ref,
    steep_ref,
    power_ref,
    bus_ref,
    adm_ref,
    off_ref,
    fwd_ref,
    inv_ref,
    wide,
    volts,
    send,
    recv,
    my_bus,
    buses,
    adm_side,
    off_side,
    weights,
    resp,
    send_back,
    load_sem,
    send_sem,
    recv_sem,
):
    me = lax.axis_index("harm")
    y = lax.axis_index("bus")
    hl = adm_ref.shape[2]
    block = adm_ref.shape[3]
    links = off_ref.shape[0]
    conv = power_ref.shape[0]
    sub = block // nh
    tiles = block // LANES
    around = LANES // sub
    rows = 8 * (around + 2)
    has_left = y > 0
    has_right = y < ny - 1
    send_right = jnp.logical_and(has_right, me == nh - 1)
    send_left = jnp.logical_and(has_left, me == 0)

    pairs = (
        (volt_hbm, volt_ref),
        (fwd_hbm, fwd_ref),
        (type_hbm, type_ref),
        (steep_hbm, steep_ref),
        (power_hbm, power_ref),
        (inv_hbm, inv_ref),
        (bus_hbm, bus_ref),
        (adm_hbm, adm_ref),
        (off_hbm, off_ref),
    )
    loads = [pltpu.make_async_copy(src, dst, load_sem.at[i]) for i, (src, dst) in enumerate(pairs)]
    for load in loads:
        load.start()

    barrier = pltpu.get_barrier_semaphore()

    def greet(d, by):
        pl.semaphore_signal(barrier, inc=1, device_id={"harm": d, "bus": by})

    def each(low, body):
        def step(i, carry):
            body(i)
            return carry

        lax.fori_loop(low, nh, step, 0)

    def peer(s):
        return lax.rem(me + s, nh)

    each(1, lambda s: greet(peer(s), y))

    @pl.when(has_left)
    def _():
        each(0, lambda d: greet(d, y - 1))

    @pl.when(has_right)
    def _():
        each(0, lambda d: greet(d, y + 1))

    @pl.when(jnp.logical_not(has_left))
    def _():
        recv[0] = jnp.zeros(recv.shape[1:], recv.dtype)
        buses[0] = jnp.zeros(buses.shape[1:], buses.dtype)
        adm_side[0] = jnp.zeros(adm_side.shape[1:], adm_side.dtype)
        off_side[0] = jnp.zeros(off_side.shape[1:], off_side.dtype)

    @pl.when(jnp.logical_not(has_right))
    def _():
        recv[nh + 1] = jnp.zeros(recv.shape[1:], recv.dtype)
        buses[nh + 1] = jnp.zeros(buses.shape[1:], buses.dtype)
        adm_side[1] = jnp.zeros(adm_side.shape[1:], adm_side.dtype)
        off_side[1] = jnp.zeros(off_side.shape[1:], off_side.dtype)

    for load in loads[:6]:
        load.wait()
    span = volt_ref.shape[0] // conv
    wide[0 : span * conv] = volt_ref[...].astype(jnp.float32)
    for c in range(conv):
        volts[:, LANES * c : LANES * (c + 1)] = wide[pl.ds(c, span, stride=conv), :].astype(jnp.bfloat16)

    def steepness(c):
        value = steep_ref[0]
        for kind in range(1, steep_ref.shape[0]):
            value = jnp.where(type_ref[c] == kind, steep_ref[kind], value)
        return jnp.full((1, LANES), value, jnp.float32)

    steep = jnp.concatenate([steepness(c) for c in range(conv)], axis=1)
    power = jnp.concatenate([power_ref[c : c + 1, :] for c in range(conv)], axis=1) * NT ** (-0.5)
    part = NT // CHUNKS
    spectra = jnp.zeros((span, conv * LANES), jnp.float32)
    for q in range(CHUNKS):
        wave = jnp.dot(fwd_ref[part * q : part * (q + 1), :], volts[...], preferred_element_type=jnp.float32)
        now = jnp.tanh(steep * wave).astype(jnp.bfloat16)
        spectra = spectra + jnp.dot(
            inv_ref[:, part * q : part * (q + 1)], now, preferred_element_type=jnp.float32
        )
    spectra = spectra * power
    for c in range(conv):
        wide[pl.ds(c, span, stride=conv), :] = spectra[:, LANES * c : LANES * (c + 1)]
    send[...] = wide[0 : span * conv].reshape(nh, hl, 8, LANES).astype(jnp.bfloat16)

    for load in loads[6:]:
        load.wait()
    first = (y * nh + me) * sub
    row8 = lax.broadcasted_iota(jnp.int32, (8, LANES), 0) % conv
    numbers = jnp.zeros((8, LANES), jnp.float32)
    for c in range(conv):
        numbers = jnp.where(row8 == c, (bus_ref[c] - first).astype(jnp.float32), numbers)
    my_bus[...] = numbers.astype(jnp.bfloat16)

    pl.semaphore_wait(barrier, nh - 1 + nh * has_left.astype(jnp.int32) + nh * has_right.astype(jnp.int32))

    def remote(src, dst, out, into, d, by):
        return pltpu.make_async_remote_copy(
            src_ref=src,
            dst_ref=dst,
            send_sem=send_sem.at[out],
            recv_sem=recv_sem.at[into],
            device_id={"harm": d, "bus": by},
        )

    def bus_copy(d, slot, by, out, into):
        return remote(my_bus, buses.at[slot], out, into, d, by)

    def spec_copy(d, slot, by, out, into):
        return remote(send.at[d], recv.at[slot], out, into, d, by)

    def ret_copy(d, source):
        place = next_ref.at[:, pl.ds(source * hl, hl)]
        return remote(send_back.at[d], place, 6, 6, d, y)

    def side_copies(side):
        by = y + 1 if side == 0 else y - 1
        start = block - LANES if side == 0 else 0
        return (
            remote(adm_ref.at[:, :, :, pl.ds(start, LANES)], adm_side.at[side], 7 + side, 7 + side, me, by),
            remote(off_ref.at[:, pl.ds(start, LANES)], off_side.at[side], 9 + side, 9 + side, me, by),
        )

    @pl.when(has_right)
    def _():
        for copy in side_copies(0):
            copy.start()

    @pl.when(has_left)
    def _():
        for copy in side_copies(1):
            copy.start()

    each(1, lambda s: bus_copy(peer(s), me + 1, y, 0, 0).start())
    each(1, lambda s: spec_copy(peer(s), me + 1, y, 3, 3).start())

    @pl.when(send_right)
    def _():
        each(0, lambda d: bus_copy(d, 0, y + 1, 1, 1).start())
        each(0, lambda d: spec_copy(d, 0, y + 1, 4, 4).start())

    @pl.when(send_left)
    def _():
        each(0, lambda d: bus_copy(d, nh + 1, y - 1, 2, 2).start())
        each(0, lambda d: spec_copy(d, nh + 1, y - 1, 5, 5).start())

    recv[me + 1] = send[me]
    buses[me + 1] = my_bus[...]

    lane = lax.broadcasted_iota(jnp.int32, (1, LANES), 1)
    is_right = lane < LANES // 2

    def adm_row(p, k, h, t, beyond):
        def row_of(t):
            if t < 0:
                return adm_side[0, p, k, h : h + 1, :]
            if t >= tiles:
                return adm_side[1, p, k, h : h + 1, :]
            return adm_ref[p, k, h : h + 1, LANES * t : LANES * (t + 1)]

        return jnp.where(is_right, row_of(t + 1), row_of(t - 1)) if beyond else row_of(t)

    def off_row(k, t, beyond):
        def row_of(t):
            if t < 0:
                return off_side[0, k : k + 1, :]
            if t >= tiles:
                return off_side[1, k : k + 1, :]
            return off_ref[k : k + 1, LANES * t : LANES * (t + 1)]

        return jnp.where(is_right, row_of(t + 1), row_of(t - 1)) if beyond else row_of(t)

    def fill(t, beyond, low, high):
        band = lax.broadcasted_iota(jnp.int32, (high - low, LANES), 0) + low
        shift = LANES if beyond else 0
        masks = [
            band == jnp.bitwise_and(lane + shift + off_row(k, t, beyond), 2 * LANES - 1) for k in range(links)
        ]
        for h in range(hl):
            d_real, d_imag = adm_row(0, 0, h, t, beyond), adm_row(1, 0, h, t, beyond)
            total_real = jnp.zeros(band.shape, jnp.float32)
            total_imag = jnp.zeros(band.shape, jnp.float32)
            for k in range(links):
                l_real, l_imag = adm_row(0, 1 + k, h, t, beyond), adm_row(1, 1 + k, h, t, beyond)
                total_real += jnp.where(masks[k], d_real * l_real - d_imag * l_imag, 0.0)
                total_imag += jnp.where(masks[k], d_real * l_imag + d_imag * l_real, 0.0)
            weights[h, t, low:high, shift : shift + LANES] = total_real.astype(jnp.bfloat16)
            weights[h, t, low:high, shift + 2 * LANES : shift + 3 * LANES] = total_imag.astype(jnp.bfloat16)

    for t in range(tiles):
        fill(t, False, 0, LANES + 16)
        fill(t, False, 2 * LANES - 16, 2 * LANES)
        for h in range(hl):
            weights[h, t, LANES + 16 : 2 * LANES - 16, :] = jnp.zeros((LANES - 32, 4 * LANES), jnp.bfloat16)
            for at in (LANES, 3 * LANES):
                weights[h, t, 16 : LANES - 16, at : at + LANES] = jnp.zeros((LANES - 32, LANES), jnp.bfloat16)

    @pl.when(has_left)
    def _():
        for copy in side_copies(0):
            copy.wait_recv()

    @pl.when(has_right)
    def _():
        for copy in side_copies(1):
            copy.wait_recv()

    for t in range(tiles):
        for low, high in ((LANES - 16, LANES + 16), (2 * LANES - 16, 2 * LANES), (0, 16)):
            fill(t, True, low, high)

    def all_of(ref, count, out, into):
        return remote(ref.at[pl.ds(0, count)], ref.at[pl.ds(0, count)], out, into, me, y)

    across = (((1,), (1,)), ((), ()))
    eye = jnp.where(lax.broadcasted_iota(jnp.int32, (LANES, LANES), 0) == lane, 1.0, 0.0)
    unit = jnp.concatenate([eye, jnp.zeros((LANES, LANES), jnp.float32)], axis=1)
    for t in range(tiles):
        for h in range(hl):
            own = jnp.concatenate(
                [weights[h, t, :, 0:LANES], weights[h, t, :, 2 * LANES : 3 * LANES]], axis=0
            )
            flipped = lax.dot_general(eye.astype(jnp.bfloat16), own, across, preferred_element_type=jnp.float32)
            step = jnp.concatenate([unit + flipped[:, : 2 * LANES], flipped[:, 2 * LANES :]], axis=0)
            step = step.astype(jnp.bfloat16)
            by_real = lax.dot_general(
                step, weights[h, t, :, 0 : 2 * LANES], across, preferred_element_type=jnp.float32
            )
            by_imag = lax.dot_general(
                step, weights[h, t, :, 2 * LANES :], across, preferred_element_type=jnp.float32
            )
            real = unit + by_real[:LANES] - by_imag[LANES:]
            imag = by_imag[:LANES] + by_real[LANES:]
            d_real = jnp.concatenate([adm_row(0, 0, h, t, False), adm_row(0, 0, h, t, True)], axis=1)
            d_imag = jnp.concatenate([adm_row(1, 0, h, t, False), adm_row(1, 0, h, t, True)], axis=1)
            resp[h, t, 0:LANES] = (real * d_real - imag * d_imag).astype(jnp.bfloat16)
            resp[h, t, LANES:] = (real * d_imag + imag * d_real).astype(jnp.bfloat16)

    all_of(buses, nh - 1, 0, 0).wait_recv()

    @pl.when(has_left)
    def _():
        bus_copy(0, 0, y, 1, 1).wait_recv()

    @pl.when(has_right)
    def _():
        bus_copy(0, nh + 1, y, 2, 2).wait_recv()

    row = lax.broadcasted_iota(jnp.int32, (rows, LANES), 0)
    is_real = row % 8 < conv
    base = jnp.bitwise_and((row // 8 - 1) * sub, 2 * LANES - 1)
    own = 8 * around
    spread, gather = [], []
    for t in range(tiles):
        near = buses[around * t : around * (t + 1) + 2].astype(jnp.float32).reshape(rows, LANES)
        at_bus = base + near.astype(jnp.int32)
        hits = [jnp.where(at_bus == lane + shift, 1.0, 0.0) for shift in (0, LANES)]
        spread.append(jnp.concatenate([hit.T for hit in hits], axis=0).astype(jnp.bfloat16))
        picks = [jnp.where(is_real, hits[0], 0.0), jnp.where(is_real, 0.0, hits[0])]
        gather.append(jnp.concatenate(picks, axis=1)[8 : 8 + own].astype(jnp.bfloat16))

    all_of(recv, nh - 1, 3, 3).wait_recv()

    @pl.when(has_left)
    def _():
        spec_copy(0, 0, y, 4, 4).wait_recv()

    @pl.when(has_right)
    def _():
        spec_copy(0, nh + 1, y, 5, 5).wait_recv()

    for t in range(tiles):
        for h in range(hl):
            here = recv[around * t : around * (t + 1) + 2, h].astype(jnp.float32).reshape(rows, LANES)
            parts = jnp.concatenate([jnp.where(is_real, here, 0.0), jnp.where(is_real, 0.0, here)], axis=1)
            injected = jnp.dot(spread[t], parts.astype(jnp.bfloat16), preferred_element_type=jnp.float32)
            solved = jnp.dot(resp[h, t], injected.astype(jnp.bfloat16), preferred_element_type=jnp.float32)
            real = solved[:LANES, :LANES] - solved[LANES:, LANES:]
            imag = solved[:LANES, LANES:] + solved[LANES:, :LANES]
            volt = jnp.concatenate([real, imag], axis=0).astype(jnp.bfloat16)
            out_ref[:, h, LANES * t : LANES * (t + 1)] = volt.reshape(2, LANES, LANES)
            at_conv = jnp.dot(gather[t], volt, preferred_element_type=jnp.float32)
            at_conv = at_conv.reshape(around, 2, conv, LANES).astype(jnp.bfloat16)
            send_back[around * t : around * (t + 1), :, h] = at_conv
    each(1, lambda s: ret_copy(peer(s), me).start())
    next_ref[:, pl.ds(me * hl, hl)] = send_back[me]

    all_of(buses, nh - 1, 0, 0).wait_send()
    all_of(recv, nh - 1, 3, 3).wait_send()

    @pl.when(has_right)
    def _():
        for copy in side_copies(0):
            copy.wait_send()

    @pl.when(has_left)
    def _():
        for copy in side_copies(1):
            copy.wait_send()

    @pl.when(send_right)
    def _():
        all_of(buses, nh, 1, 1).wait_send()
        all_of(recv, nh, 4, 4).wait_send()

    @pl.when(send_left)
    def _():
        all_of(buses, nh, 2, 2).wait_send()
        all_of(recv, nh, 5, 5).wait_send()

    all_of(send_back, nh - 1, 6, 6).wait_send()
    all_of(send_back, nh - 1, 6, 6).wait_recv()


def store(volt_ref, next_ref, volt_out, next_out, sems):
    copies = [pltpu.make_async_copy(volt_ref.at[p], volt_out.at[p], sems.at[p]) for p in range(2)]
    copies.append(pltpu.make_async_copy(next_ref, next_out, sems.at[2]))
    for copy in copies:
        copy.start()
    for copy in copies:
        copy.wait()


def local(nh, ny, conv_volt, conv_power, conv_type, type_steep, conv_bus, admittance, link_offset):
    _, orders, conv, snaps = conv_volt.shape
    hl = orders // nh
    block = admittance.shape[3]
    tiles = block // LANES
    around = LANES * nh // block
    span = 2 * orders
    basis = make_basis(orders)
    regrouped = basis.reshape(2, orders, NT).transpose(1, 0, 2).reshape(span, NT)
    vmem = pl.BlockSpec(memory_space=pltpu.VMEM)
    anywhere = pl.BlockSpec(memory_space=pl.ANY)
    bf16 = jnp.bfloat16
    dma = pltpu.SemaphoreType.DMA
    volt_shape, next_shape = (2, hl, block, snaps), (2, orders, conv, snaps)
    solved = pl.pallas_call(
        functools.partial(kernel, nh, ny),
        out_shape=(pltpu.VMEM(volt_shape, bf16), pltpu.VMEM(next_shape, bf16)),
        in_specs=[anywhere] * 9,
        out_specs=(vmem, vmem),
        scratch_shapes=[
            pltpu.VMEM((span * conv, snaps), bf16),
            pltpu.SMEM(conv_type.shape, jnp.int32),
            pltpu.SMEM(type_steep.shape, jnp.float32),
            pltpu.VMEM((conv, snaps), jnp.float32),
            pltpu.SMEM(conv_bus.shape, jnp.int32),
            pltpu.VMEM(admittance.shape, jnp.float32),
            pltpu.VMEM(link_offset.shape, jnp.int32),
            pltpu.VMEM((NT, span), bf16),
            pltpu.VMEM((span, NT), bf16),
            pltpu.VMEM((span * conv + 8, LANES), jnp.float32),
            pltpu.VMEM((span, conv * LANES), bf16),
            pltpu.VMEM((nh, hl, 8, LANES), bf16),
            pltpu.VMEM((nh + 2, hl, 8, LANES), bf16),
            pltpu.VMEM((8, LANES), bf16),
            pltpu.VMEM((nh + 2, 8, LANES), bf16),
            pltpu.VMEM((2,) + admittance.shape[:3] + (LANES,), jnp.float32),
            pltpu.VMEM((2, link_offset.shape[0], LANES), jnp.int32),
            pltpu.VMEM((hl, tiles, 2 * LANES, 4 * LANES), bf16),
            pltpu.VMEM((hl, tiles, 2 * LANES, 2 * LANES), bf16),
            pltpu.VMEM((nh, 2, hl, conv, LANES), bf16),
            dma((9,)),
            dma((11,)),
            dma((11,)),
        ],
        compiler_params=pltpu.CompilerParams(collective_id=0, has_side_effects=True, vmem_limit_bytes=56 * 2**20),
        name="power_flow",
    )(
        conv_volt.reshape(span * conv, snaps),
        conv_power,
        conv_type,
        type_steep,
        conv_bus,
        admittance,
        link_offset,
        jnp.asarray(basis.T, bf16),
        jnp.asarray(regrouped, bf16),
    )
    return pl.pallas_call(
        store,
        out_shape=(jax.ShapeDtypeStruct(volt_shape, bf16), jax.ShapeDtypeStruct(next_shape, bf16)),
        in_specs=[vmem, vmem],
        out_specs=(anywhere, anywhere),
        scratch_shapes=[dma((3,))],
        compiler_params=pltpu.CompilerParams(vmem_limit_bytes=32 * 2**20),
        name="store_results",
    )(*solved)


def solution(mesh):
    in_specs = (
        P(None, None, ("bus", "harm"), None),
        P(("bus", "harm"), None),
        P(("bus", "harm")),
        P(),
        P(("bus", "harm")),
        P(None, None, "harm", "bus"),
        P(None, "bus"),
    )
    out_specs = (P(None, "harm", "bus", None), P(None, None, ("bus", "harm"), None))
    body = functools.partial(local, mesh.shape["harm"], mesh.shape["bus"])
    return jax.shard_map(body, mesh=mesh, in_specs=in_specs, out_specs=out_specs, check_vma=False)
```

```python
import functools
import math

import jax
import jax.numpy as jnp
import numpy as np
from jax import lax
from jax.experimental import pallas as pl
from jax.experimental.pallas import tpu as pltpu
from jax.sharding import PartitionSpec as P

NT = 1024
LANES = 128
CHUNKS = 4


def make_basis(orders):
    samples = np.arange(NT)
    phases = (np.arange(1, orders + 1)[:, None] * samples[None, :] % NT) * (2.0 * math.pi / NT)
    return np.concatenate([np.cos(phases), -np.sin(phases)], axis=0).astype(np.float32)


def kernel(
    nh,
    ny,
    volt_hbm,
    power_hbm,
    type_hbm,
    steep_hbm,
    bus_hbm,
    adm_hbm,
    off_hbm,
    fwd_hbm,
    inv_hbm,
    out_ref,
    next_ref,
    volt_ref,
    type_ref,
    steep_ref,
    power_ref,
    bus_ref,
    adm_ref,
    off_ref,
    fwd_ref,
    inv_ref,
    wide,
    volts,
    send,
    recv,
    my_bus,
    buses,
    adm_side,
    off_side,
    weights,
    resp,
    send_back,
    load_sem,
    send_sem,
    recv_sem,
):
    me = lax.axis_index("harm")
    y = lax.axis_index("bus")
    hl = adm_ref.shape[2]
    block = adm_ref.shape[3]
    links = off_ref.shape[0]
    conv = power_ref.shape[0]
    sub = block // nh
    tiles = block // LANES
    around = LANES // sub
    rows = 8 * (around + 2)
    has_left = y > 0
    has_right = y < ny - 1
    send_right = jnp.logical_and(has_right, me == nh - 1)
    send_left = jnp.logical_and(has_left, me == 0)

    pairs = (
        (volt_hbm, volt_ref),
        (fwd_hbm, fwd_ref),
        (type_hbm, type_ref),
        (steep_hbm, steep_ref),
        (power_hbm, power_ref),
        (inv_hbm, inv_ref),
        (bus_hbm, bus_ref),
        (adm_hbm, adm_ref),
        (off_hbm, off_ref),
    )
    loads = [pltpu.make_async_copy(src, dst, load_sem.at[i]) for i, (src, dst) in enumerate(pairs)]
    for load in loads:
        load.start()

    barrier = pltpu.get_barrier_semaphore()

    def greet(d, by):
        pl.semaphore_signal(barrier, inc=1, device_id={"harm": d, "bus": by})

    def each(low, body):
        def step(i, carry):
            body(i)
            return carry

        lax.fori_loop(low, nh, step, 0)

    def peer(s):
        return lax.rem(me + s, nh)

    each(1, lambda s: greet(peer(s), y))

    @pl.when(has_left)
    def _():
        each(0, lambda d: greet(d, y - 1))

    @pl.when(has_right)
    def _():
        each(0, lambda d: greet(d, y + 1))

    @pl.when(jnp.logical_not(has_left))
    def _():
        recv[0] = jnp.zeros(recv.shape[1:], recv.dtype)
        buses[0] = jnp.zeros(buses.shape[1:], buses.dtype)
        adm_side[0] = jnp.zeros(adm_side.shape[1:], adm_side.dtype)
        off_side[0] = jnp.zeros(off_side.shape[1:], off_side.dtype)

    @pl.when(jnp.logical_not(has_right))
    def _():
        recv[nh + 1] = jnp.zeros(recv.shape[1:], recv.dtype)
        buses[nh + 1] = jnp.zeros(buses.shape[1:], buses.dtype)
        adm_side[1] = jnp.zeros(adm_side.shape[1:], adm_side.dtype)
        off_side[1] = jnp.zeros(off_side.shape[1:], off_side.dtype)

    for load in loads[:6]:
        load.wait()
    span = volt_ref.shape[0] // conv
    wide[0 : span * conv] = volt_ref[...].astype(jnp.float32)
    for c in range(conv):
        volts[:, LANES * c : LANES * (c + 1)] = wide[pl.ds(c, span, stride=conv), :].astype(jnp.bfloat16)

    def steepness(c):
        value = steep_ref[0]
        for kind in range(1, steep_ref.shape[0]):
            value = jnp.where(type_ref[c] == kind, steep_ref[kind], value)
        return jnp.full((1, LANES), value, jnp.float32)

    steep = jnp.concatenate([steepness(c) for c in range(conv)], axis=1)
    power = jnp.concatenate([power_ref[c : c + 1, :] for c in range(conv)], axis=1) * NT ** (-0.5)
    part = NT // CHUNKS
    spectra = jnp.zeros((span, conv * LANES), jnp.float32)
    for q in range(CHUNKS):
        wave = jnp.dot(fwd_ref[part * q : part * (q + 1), :], volts[...], preferred_element_type=jnp.float32)
        now = jnp.tanh(steep * wave).astype(jnp.bfloat16)
        spectra = spectra + jnp.dot(
            inv_ref[:, part * q : part * (q + 1)], now, preferred_element_type=jnp.float32
        )
    spectra = spectra * power
    for c in range(conv):
        wide[pl.ds(c, span, stride=conv), :] = spectra[:, LANES * c : LANES * (c + 1)]
    send[...] = wide[0 : span * conv].reshape(nh, hl, 8, LANES).astype(jnp.bfloat16)

    for load in loads[6:]:
        load.wait()
    first = (y * nh + me) * sub
    row8 = lax.broadcasted_iota(jnp.int32, (8, LANES), 0) % conv
    numbers = jnp.zeros((8, LANES), jnp.float32)
    for c in range(conv):
        numbers = jnp.where(row8 == c, (bus_ref[c] - first).astype(jnp.float32), numbers)
    my_bus[...] = numbers.astype(jnp.bfloat16)

    pl.semaphore_wait(barrier, nh - 1 + nh * has_left.astype(jnp.int32) + nh * has_right.astype(jnp.int32))

    def remote(src, dst, out, into, d, by):
        return pltpu.make_async_remote_copy(
            src_ref=src,
            dst_ref=dst,
            send_sem=send_sem.at[out],
            recv_sem=recv_sem.at[into],
            device_id={"harm": d, "bus": by},
        )

    def bus_copy(d, slot, by, out, into):
        return remote(my_bus, buses.at[slot], out, into, d, by)

    def spec_copy(d, slot, by, out, into):
        return remote(send.at[d], recv.at[slot], out, into, d, by)

    def ret_copy(d, source):
        place = next_ref.at[:, pl.ds(source * hl, hl)]
        return remote(send_back.at[d], place, 6, 6, d, y)

    def side_copies(side):
        by = y + 1 if side == 0 else y - 1
        start = block - LANES if side == 0 else 0
        return (
            remote(adm_ref.at[:, :, :, pl.ds(start, LANES)], adm_side.at[side], 7 + side, 7 + side, me, by),
            remote(off_ref.at[:, pl.ds(start, LANES)], off_side.at[side], 9 + side, 9 + side, me, by),
        )

    @pl.when(has_right)
    def _():
        for copy in side_copies(0):
            copy.start()

    @pl.when(has_left)
    def _():
        for copy in side_copies(1):
            copy.start()

    each(1, lambda s: bus_copy(peer(s), me + 1, y, 0, 0).start())
    each(1, lambda s: spec_copy(peer(s), me + 1, y, 3, 3).start())

    @pl.when(send_right)
    def _():
        each(0, lambda d: bus_copy(d, 0, y + 1, 1, 1).start())
        each(0, lambda d: spec_copy(d, 0, y + 1, 4, 4).start())

    @pl.when(send_left)
    def _():
        each(0, lambda d: bus_copy(d, nh + 1, y - 1, 2, 2).start())
        each(0, lambda d: spec_copy(d, nh + 1, y - 1, 5, 5).start())

    recv[me + 1] = send[me]
    buses[me + 1] = my_bus[...]

    lane = lax.broadcasted_iota(jnp.int32, (1, LANES), 1)
    is_right = lane < LANES // 2

    def adm_row(p, k, h, t, beyond):
        def row_of(t):
            if t < 0:
                return adm_side[0, p, k, h : h + 1, :]
            if t >= tiles:
                return adm_side[1, p, k, h : h + 1, :]
            return adm_ref[p, k, h : h + 1, LANES * t : LANES * (t + 1)]

        return jnp.where(is_right, row_of(t + 1), row_of(t - 1)) if beyond else row_of(t)

    def off_row(k, t, beyond):
        def row_of(t):
            if t < 0:
                return off_side[0, k : k + 1, :]
            if t >= tiles:
                return off_side[1, k : k + 1, :]
            return off_ref[k : k + 1, LANES * t : LANES * (t + 1)]

        return jnp.where(is_right, row_of(t + 1), row_of(t - 1)) if beyond else row_of(t)

    def fill(t, beyond, low, high):
        band = lax.broadcasted_iota(jnp.int32, (high - low, LANES), 0) + low
        shift = LANES if beyond else 0
        masks = [
            band == jnp.bitwise_and(lane + shift + off_row(k, t, beyond), 2 * LANES - 1) for k in range(links)
        ]
        for h in range(hl):
            d_real, d_imag = adm_row(0, 0, h, t, beyond), adm_row(1, 0, h, t, beyond)
            total_real = jnp.zeros(band.shape, jnp.float32)
            total_imag = jnp.zeros(band.shape, jnp.float32)
            for k in range(links):
                l_real, l_imag = adm_row(0, 1 + k, h, t, beyond), adm_row(1, 1 + k, h, t, beyond)
                total_real += jnp.where(masks[k], d_real * l_real - d_imag * l_imag, 0.0)
                total_imag += jnp.where(masks[k], d_real * l_imag + d_imag * l_real, 0.0)
            weights[h, t, low:high, shift : shift + LANES] = total_real.astype(jnp.bfloat16)
            weights[h, t, low:high, shift + 2 * LANES : shift + 3 * LANES] = total_imag.astype(jnp.bfloat16)

    for t in range(tiles):
        fill(t, False, 0, LANES + 16)
        fill(t, False, 2 * LANES - 16, 2 * LANES)
        for h in range(hl):
            weights[h, t, LANES + 16 : 2 * LANES - 16, :] = jnp.zeros((LANES - 32, 4 * LANES), jnp.bfloat16)
            for at in (LANES, 3 * LANES):
                weights[h, t, 16 : LANES - 16, at : at + LANES] = jnp.zeros((LANES - 32, LANES), jnp.bfloat16)

    @pl.when(has_left)
    def _():
        for copy in side_copies(0):
            copy.wait_recv()

    @pl.when(has_right)
    def _():
        for copy in side_copies(1):
            copy.wait_recv()

    for t in range(tiles):
        for low, high in ((LANES - 16, LANES + 16), (2 * LANES - 16, 2 * LANES), (0, 16)):
            fill(t, True, low, high)

    def all_of(ref, count, out, into):
        return remote(ref.at[pl.ds(0, count)], ref.at[pl.ds(0, count)], out, into, me, y)

    across = (((1,), (1,)), ((), ()))
    eye = jnp.where(lax.broadcasted_iota(jnp.int32, (LANES, LANES), 0) == lane, 1.0, 0.0)
    unit = jnp.concatenate([eye, jnp.zeros((LANES, LANES), jnp.float32)], axis=1)
    for t in range(tiles):
        for h in range(hl):
            own = jnp.concatenate(
                [weights[h, t, :, 0:LANES], weights[h, t, :, 2 * LANES : 3 * LANES]], axis=0
            )
            flipped = lax.dot_general(eye.astype(jnp.bfloat16), own, across, preferred_element_type=jnp.float32)
            step = jnp.concatenate([unit + flipped[:, : 2 * LANES], flipped[:, 2 * LANES :]], axis=0)
            step = step.astype(jnp.bfloat16)
            by_real = lax.dot_general(
                step, weights[h, t, :, 0 : 2 * LANES], across, preferred_element_type=jnp.float32
            )
            by_imag = lax.dot_general(
                step, weights[h, t, :, 2 * LANES :], across, preferred_element_type=jnp.float32
            )
            real = unit + by_real[:LANES] - by_imag[LANES:]
            imag = by_imag[:LANES] + by_real[LANES:]
            d_real = jnp.concatenate([adm_row(0, 0, h, t, False), adm_row(0, 0, h, t, True)], axis=1)
            d_imag = jnp.concatenate([adm_row(1, 0, h, t, False), adm_row(1, 0, h, t, True)], axis=1)
            resp[h, t, 0:LANES] = (real * d_real - imag * d_imag).astype(jnp.bfloat16)
            resp[h, t, LANES:] = (real * d_imag + imag * d_real).astype(jnp.bfloat16)

    all_of(buses, nh - 1, 0, 0).wait_recv()

    @pl.when(has_left)
    def _():
        bus_copy(0, 0, y, 1, 1).wait_recv()

    @pl.when(has_right)
    def _():
        bus_copy(0, nh + 1, y, 2, 2).wait_recv()

    row = lax.broadcasted_iota(jnp.int32, (rows, LANES), 0)
    is_real = row % 8 < conv
    base = jnp.bitwise_and((row // 8 - 1) * sub, 2 * LANES - 1)
    own = 8 * around
    spread, gather = [], []
    for t in range(tiles):
        near = buses[around * t : around * (t + 1) + 2].astype(jnp.float32).reshape(rows, LANES)
        at_bus = base + near.astype(jnp.int32)
        hits = [jnp.where(at_bus == lane + shift, 1.0, 0.0) for shift in (0, LANES)]
        spread.append(jnp.concatenate([hit.T for hit in hits], axis=0).astype(jnp.bfloat16))
        picks = [jnp.where(is_real, hits[0], 0.0), jnp.where(is_real, 0.0, hits[0])]
        gather.append(jnp.concatenate(picks, axis=1)[8 : 8 + own].astype(jnp.bfloat16))

    all_of(recv, nh - 1, 3, 3).wait_recv()

    @pl.when(has_left)
    def _():
        spec_copy(0, 0, y, 4, 4).wait_recv()

    @pl.when(has_right)
    def _():
        spec_copy(0, nh + 1, y, 5, 5).wait_recv()

    injected, solved, volts_now = [], [], []
    for t in range(tiles):
        parts = []
        for h in range(hl):
            here = recv[around * t : around * (t + 1) + 2, h].astype(jnp.float32).reshape(rows, LANES)
            parts += [jnp.where(is_real, here, 0.0), jnp.where(is_real, 0.0, here)]
        parts = jnp.concatenate(parts, axis=1).astype(jnp.bfloat16)
        injected.append(jnp.dot(spread[t], parts, preferred_element_type=jnp.float32).astype(jnp.bfloat16))
    for t in range(tiles):
        for h in range(hl):
            mine = injected[t][:, 2 * LANES * h : 2 * LANES * (h + 1)]
            solved.append(jnp.dot(resp[h, t], mine, preferred_element_type=jnp.float32))
    for t in range(tiles):
        now = []
        for h in range(hl):
            both = solved[t * hl + h]
            real = both[:LANES, :LANES] - both[LANES:, LANES:]
            imag = both[:LANES, LANES:] + both[LANES:, :LANES]
            now.append(jnp.concatenate([real, imag], axis=0).astype(jnp.bfloat16))
        volts_now.append(now)
        at_conv = jnp.dot(gather[t], jnp.concatenate(now, axis=1), preferred_element_type=jnp.float32)
        for h in range(hl):
            chosen = at_conv[:, LANES * h : LANES * (h + 1)].reshape(around, 2, conv, LANES)
            send_back[around * t : around * (t + 1), :, h] = chosen.astype(jnp.bfloat16)
    each(1, lambda s: ret_copy(peer(s), me).start())
    next_ref[:, pl.ds(me * hl, hl)] = send_back[me]
    for t in range(tiles):
        for h in range(hl):
            out_ref[:, h, LANES * t : LANES * (t + 1)] = volts_now[t][h].reshape(2, LANES, LANES)

    all_of(buses, nh - 1, 0, 0).wait_send()
    all_of(recv, nh - 1, 3, 3).wait_send()

    @pl.when(has_right)
    def _():
        for copy in side_copies(0):
            copy.wait_send()

    @pl.when(has_left)
    def _():
        for copy in side_copies(1):
            copy.wait_send()

    @pl.when(send_right)
    def _():
        all_of(buses, nh, 1, 1).wait_send()
        all_of(recv, nh, 4, 4).wait_send()

    @pl.when(send_left)
    def _():
        all_of(buses, nh, 2, 2).wait_send()
        all_of(recv, nh, 5, 5).wait_send()

    all_of(send_back, nh - 1, 6, 6).wait_send()
    all_of(send_back, nh - 1, 6, 6).wait_recv()


def store(volt_ref, next_ref, volt_out, next_out, sems):
    copies = [pltpu.make_async_copy(volt_ref.at[p], volt_out.at[p], sems.at[p]) for p in range(2)]
    copies.append(pltpu.make_async_copy(next_ref, next_out, sems.at[2]))
    for copy in copies:
        copy.start()
    for copy in copies:
        copy.wait()


def local(nh, ny, conv_volt, conv_power, conv_type, type_steep, conv_bus, admittance, link_offset):
    _, orders, conv, snaps = conv_volt.shape
    hl = orders // nh
    block = admittance.shape[3]
    tiles = block // LANES
    around = LANES * nh // block
    span = 2 * orders
    basis = make_basis(orders)
    regrouped = basis.reshape(2, orders, NT).transpose(1, 0, 2).reshape(span, NT)
    vmem = pl.BlockSpec(memory_space=pltpu.VMEM)
    anywhere = pl.BlockSpec(memory_space=pl.ANY)
    bf16 = jnp.bfloat16
    dma = pltpu.SemaphoreType.DMA
    volt_shape, next_shape = (2, hl, block, snaps), (2, orders, conv, snaps)
    solved = pl.pallas_call(
        functools.partial(kernel, nh, ny),
        out_shape=(pltpu.VMEM(volt_shape, bf16), pltpu.VMEM(next_shape, bf16)),
        in_specs=[anywhere] * 9,
        out_specs=(vmem, vmem),
        scratch_shapes=[
            pltpu.VMEM((span * conv, snaps), bf16),
            pltpu.SMEM(conv_type.shape, jnp.int32),
            pltpu.SMEM(type_steep.shape, jnp.float32),
            pltpu.VMEM((conv, snaps), jnp.float32),
            pltpu.SMEM(conv_bus.shape, jnp.int32),
            pltpu.VMEM(admittance.shape, jnp.float32),
            pltpu.VMEM(link_offset.shape, jnp.int32),
            pltpu.VMEM((NT, span), bf16),
            pltpu.VMEM((span, NT), bf16),
            pltpu.VMEM((span * conv + 8, LANES), jnp.float32),
            pltpu.VMEM((span, conv * LANES), bf16),
            pltpu.VMEM((nh, hl, 8, LANES), bf16),
            pltpu.VMEM((nh + 2, hl, 8, LANES), bf16),
            pltpu.VMEM((8, LANES), bf16),
            pltpu.VMEM((nh + 2, 8, LANES), bf16),
            pltpu.VMEM((2,) + admittance.shape[:3] + (LANES,), jnp.float32),
            pltpu.VMEM((2, link_offset.shape[0], LANES), jnp.int32),
            pltpu.VMEM((hl, tiles, 2 * LANES, 4 * LANES), bf16),
            pltpu.VMEM((hl, tiles, 2 * LANES, 2 * LANES), bf16),
            pltpu.VMEM((nh, 2, hl, conv, LANES), bf16),
            dma((9,)),
            dma((11,)),
            dma((11,)),
        ],
        compiler_params=pltpu.CompilerParams(collective_id=0, has_side_effects=True, vmem_limit_bytes=56 * 2**20),
        name="power_flow",
    )(
        conv_volt.reshape(span * conv, snaps),
        conv_power,
        conv_type,
        type_steep,
        conv_bus,
        admittance,
        link_offset,
        jnp.asarray(basis.T, bf16),
        jnp.asarray(regrouped, bf16),
    )
    return pl.pallas_call(
        store,
        out_shape=(jax.ShapeDtypeStruct(volt_shape, bf16), jax.ShapeDtypeStruct(next_shape, bf16)),
        in_specs=[vmem, vmem],
        out_specs=(anywhere, anywhere),
        scratch_shapes=[dma((3,))],
        compiler_params=pltpu.CompilerParams(vmem_limit_bytes=32 * 2**20),
        name="store_results",
    )(*solved)


def solution(mesh):
    in_specs = (
        P(None, None, ("bus", "harm"), None),
        P(("bus", "harm"), None),
        P(("bus", "harm")),
        P(),
        P(("bus", "harm")),
        P(None, None, "harm", "bus"),
        P(None, "bus"),
    )
    out_specs = (P(None, "harm", "bus", None), P(None, None, ("bus", "harm"), None))
    body = functools.partial(local, mesh.shape["harm"], mesh.shape["bus"])
    return jax.shard_map(body, mesh=mesh, in_specs=in_specs, out_specs=out_specs, check_vma=False)
```

```python
import functools
import math

import jax
import jax.numpy as jnp
import numpy as np
from jax import lax
from jax.experimental import pallas as pl
from jax.experimental.pallas import tpu as pltpu
from jax.sharding import PartitionSpec as P

NT = 1024
LANES = 128
REACH = 8
CHUNKS = 4


def make_basis(orders):
    samples = np.arange(NT)
    phases = (np.arange(1, orders + 1)[:, None] * samples[None, :] % NT) * (2.0 * math.pi / NT)
    return np.concatenate([np.cos(phases), -np.sin(phases)], axis=0).astype(np.float32)


def kernel(
    nh,
    ny,
    volt_hbm,
    power_hbm,
    type_hbm,
    steep_hbm,
    bus_hbm,
    adm_hbm,
    off_hbm,
    fwd_hbm,
    inv_hbm,
    out_ref,
    next_ref,
    volt_ref,
    type_ref,
    steep_ref,
    power_ref,
    bus_ref,
    adm_ref,
    off_ref,
    fwd_ref,
    inv_ref,
    wide,
    volts,
    send,
    recv,
    my_bus,
    buses,
    adm_side,
    off_side,
    weights,
    resp,
    parcels,
    parcel_recv,
    parcel_edge,
    near_spec,
    off_row8,
    load_sem,
    send_sem,
    recv_sem,
):
    me = lax.axis_index("harm")
    y = lax.axis_index("bus")
    hl = adm_ref.shape[2]
    block = adm_ref.shape[3]
    links = off_ref.shape[0]
    conv = power_ref.shape[0]
    sub = block // nh
    tiles = block // LANES
    around = LANES // sub
    rows = 8 * (around + 2)
    deep = parcels.shape[1] // 4
    inner, outer = sub + 2 * REACH, sub + 4 * REACH
    has_left = y > 0
    has_right = y < ny - 1
    place = y * nh + me
    near_left, near_right = place > 0, place < ny * nh - 1
    send_right = jnp.logical_and(has_right, me == nh - 1)
    send_left = jnp.logical_and(has_left, me == 0)

    pairs = (
        (volt_hbm, volt_ref),
        (fwd_hbm, fwd_ref),
        (type_hbm, type_ref),
        (steep_hbm, steep_ref),
        (power_hbm, power_ref),
        (inv_hbm, inv_ref),
        (bus_hbm, bus_ref),
        (adm_hbm, adm_ref),
        (off_hbm, off_ref),
    )
    loads = [pltpu.make_async_copy(src, dst, load_sem.at[i]) for i, (src, dst) in enumerate(pairs)]
    for load in loads:
        load.start()

    barrier = pltpu.get_barrier_semaphore()

    def greet(d, by):
        pl.semaphore_signal(barrier, inc=1, device_id={"harm": d, "bus": by})

    def each(low, body):
        def step(i, carry):
            body(i)
            return carry

        lax.fori_loop(low, nh, step, 0)

    def peer(s):
        return lax.rem(me + s, nh)

    each(1, lambda s: greet(peer(s), y))

    @pl.when(has_left)
    def _():
        each(0, lambda d: greet(d, y - 1))

    @pl.when(has_right)
    def _():
        each(0, lambda d: greet(d, y + 1))

    @pl.when(jnp.logical_not(has_left))
    def _():
        recv[0] = jnp.zeros(recv.shape[1:], recv.dtype)
        buses[0] = jnp.zeros(buses.shape[1:], buses.dtype)
        adm_side[0] = jnp.zeros(adm_side.shape[1:], adm_side.dtype)
        off_side[0] = jnp.zeros(off_side.shape[1:], off_side.dtype)

    @pl.when(jnp.logical_not(has_right))
    def _():
        recv[nh + 1] = jnp.zeros(recv.shape[1:], recv.dtype)
        buses[nh + 1] = jnp.zeros(buses.shape[1:], buses.dtype)
        adm_side[1] = jnp.zeros(adm_side.shape[1:], adm_side.dtype)
        off_side[1] = jnp.zeros(off_side.shape[1:], off_side.dtype)

    @pl.when(jnp.logical_not(jnp.logical_or(send_left, send_right)))
    def _():
        parcel_edge[...] = jnp.zeros(parcel_edge.shape, parcel_edge.dtype)

    @pl.when(jnp.logical_not(near_left))
    def _():
        near_spec[0] = jnp.zeros(near_spec.shape[1:], near_spec.dtype)

    @pl.when(jnp.logical_not(near_right))
    def _():
        near_spec[1] = jnp.zeros(near_spec.shape[1:], near_spec.dtype)

    for load in loads[:6]:
        load.wait()
    span = volt_ref.shape[0] // conv
    wide[0 : span * conv] = volt_ref[...].astype(jnp.float32)
    for c in range(conv):
        volts[:, LANES * c : LANES * (c + 1)] = wide[pl.ds(c, span, stride=conv), :].astype(jnp.bfloat16)

    def steepness(c):
        value = steep_ref[0]
        for kind in range(1, steep_ref.shape[0]):
            value = jnp.where(type_ref[c] == kind, steep_ref[kind], value)
        return jnp.full((1, LANES), value, jnp.float32)

    steep = jnp.concatenate([steepness(c) for c in range(conv)], axis=1)
    power = jnp.concatenate([power_ref[c : c + 1, :] for c in range(conv)], axis=1) * NT ** (-0.5)
    part = NT // CHUNKS
    spectra = jnp.zeros((span, conv * LANES), jnp.float32)
    for q in range(CHUNKS):
        wave = jnp.dot(fwd_ref[part * q : part * (q + 1), :], volts[...], preferred_element_type=jnp.float32)
        now = jnp.tanh(steep * wave).astype(jnp.bfloat16)
        spectra = spectra + jnp.dot(
            inv_ref[:, part * q : part * (q + 1)], now, preferred_element_type=jnp.float32
        )
    spectra = spectra * power
    for c in range(conv):
        wide[pl.ds(c, span, stride=conv), :] = spectra[:, LANES * c : LANES * (c + 1)]
    send[...] = wide[0 : span * conv].reshape(nh, hl, 8, LANES).astype(jnp.bfloat16)

    for load in loads[6:]:
        load.wait()
    first = (y * nh + me) * sub
    row8 = lax.broadcasted_iota(jnp.int32, (8, LANES), 0) % conv
    numbers = jnp.zeros((8, LANES), jnp.float32)
    for c in range(conv):
        numbers = jnp.where(row8 == c, (bus_ref[c] - first).astype(jnp.float32), numbers)
    my_bus[...] = numbers.astype(jnp.bfloat16)

    lane = lax.broadcasted_iota(jnp.int32, (1, LANES), 1)

    def window(pieces, start, at):
        first_piece = start // LANES
        shift = (at - start) % LANES
        moved = []
        for piece in (first_piece, first_piece + 1):
            if 0 <= piece < len(pieces):
                moved.append(pltpu.roll(pieces[piece], shift, 1) if shift else pieces[piece])
            else:
                moved.append(jnp.zeros(pieces[0].shape, pieces[0].dtype))
        return jnp.where(lane - at < LANES * (first_piece + 1) - start, moved[0], moved[1])

    def stacked(real, imag):
        if deep == hl:
            return jnp.concatenate([real, imag], axis=0)
        empty = jnp.zeros((deep - hl, LANES), jnp.float32)
        return jnp.concatenate([real, empty, imag, empty], axis=0)

    selfs, lines = [], [[] for _ in range(links)]
    for t in range(tiles):
        cut = slice(LANES * t, LANES * (t + 1))
        d_real, d_imag = adm_ref[0, 0, :, cut], adm_ref[1, 0, :, cut]
        selfs.append(stacked(d_real, d_imag))
        for k in range(links):
            l_real, l_imag = adm_ref[0, 1 + k, :, cut], adm_ref[1, 1 + k, :, cut]
            lines[k].append(stacked(d_real * l_real - d_imag * l_imag, d_real * l_imag + d_imag * l_real))
    for m in range(-1, nh + 1):
        line_part = jnp.zeros((2 * deep, LANES), jnp.float32)
        for k in range(links):
            inside = jnp.logical_and(lane >= inner * k, lane < inner * (k + 1))
            line_part = jnp.where(inside, window(lines[k], sub * m - REACH, inner * k), line_part)
        self_part = jnp.where(lane < outer, window(selfs, sub * m - 2 * REACH, 0), 0.0)
        parcels[m + 1] = jnp.concatenate([line_part, self_part], axis=0).astype(jnp.bfloat16)

    pl.semaphore_wait(barrier, nh - 1 + nh * has_left.astype(jnp.int32) + nh * has_right.astype(jnp.int32))

    def remote(src, dst, out, into, d, by):
        return pltpu.make_async_remote_copy(
            src_ref=src,
            dst_ref=dst,
            send_sem=send_sem.at[out],
            recv_sem=recv_sem.at[into],
            device_id={"harm": d, "bus": by},
        )

    def bus_copy(d, slot, by, out, into):
        return remote(my_bus, buses.at[slot], out, into, d, by)

    def spec_copy(d, slot, by, out, into):
        return remote(send.at[d], recv.at[slot], out, into, d, by)

    def parcel_copy(d):
        return remote(parcels.at[d + 1], parcel_recv.at[me], 6, 6, d, y)

    def edge_copy(side, d, by):
        own_parcel = parcels.at[nh + 1 if side == 0 else 0]
        return remote(own_parcel, parcel_edge.at[me], 11 + side, 11, d, by)

    def near_copy(side, d, by):
        return remote(send, near_spec.at[side], 13 + side, 13 + side, d, by)

    up, down = lax.rem(y + 1, ny), lax.rem(y + ny - 1, ny)

    def side_copies(side):
        by = y + 1 if side == 0 else y - 1
        start = block - LANES if side == 0 else 0
        return (
            remote(adm_ref.at[:, :, :, pl.ds(start, LANES)], adm_side.at[side], 7 + side, 7 + side, me, by),
            remote(off_ref.at[:, pl.ds(start, LANES)], off_side.at[side], 9 + side, 9 + side, me, by),
        )

    @pl.when(has_right)
    def _():
        for copy in side_copies(0):
            copy.start()

    @pl.when(has_left)
    def _():
        for copy in side_copies(1):
            copy.start()

    each(1, lambda s: bus_copy(peer(s), me + 1, y, 0, 0).start())
    each(1, lambda s: parcel_copy(peer(s)).start())

    @pl.when(has_right)
    def _():
        edge_copy(0, lax.rem(me + nh - me, nh), up).start()

    @pl.when(has_left)
    def _():
        edge_copy(1, lax.rem(me + 2 * nh - 1 - me, nh), down).start()

    each(1, lambda s: spec_copy(peer(s), me + 1, y, 3, 3).start())

    @pl.when(me < nh - 1)
    def _():
        near_copy(0, peer(1), y).start()

    @pl.when(me > 0)
    def _():
        near_copy(1, peer(nh - 1), y).start()

    @pl.when(send_right)
    def _():
        near_copy(0, peer(1), up).start()

    @pl.when(send_left)
    def _():
        near_copy(1, peer(nh - 1), down).start()

    @pl.when(send_right)
    def _():
        each(0, lambda d: bus_copy(d, 0, y + 1, 1, 1).start())
        each(0, lambda d: spec_copy(d, 0, y + 1, 4, 4).start())

    @pl.when(send_left)
    def _():
        each(0, lambda d: bus_copy(d, nh + 1, y - 1, 2, 2).start())
        each(0, lambda d: spec_copy(d, nh + 1, y - 1, 5, 5).start())

    recv[me + 1] = send[me]
    buses[me + 1] = my_bus[...]
    parcel_recv[me] = parcels[me + 1]

    is_right = lane < LANES // 2

    def adm_row(p, k, h, t, beyond):
        def row_of(t):
            if t < 0:
                return adm_side[0, p, k, h : h + 1, :]
            if t >= tiles:
                return adm_side[1, p, k, h : h + 1, :]
            return adm_ref[p, k, h : h + 1, LANES * t : LANES * (t + 1)]

        return jnp.where(is_right, row_of(t + 1), row_of(t - 1)) if beyond else row_of(t)

    def off_row(k, t, beyond):
        def row_of(t):
            if t < 0:
                return off_side[0, k : k + 1, :]
            if t >= tiles:
                return off_side[1, k : k + 1, :]
            return off_ref[k : k + 1, LANES * t : LANES * (t + 1)]

        return jnp.where(is_right, row_of(t + 1), row_of(t - 1)) if beyond else row_of(t)

    def fill(t, beyond, low, high):
        band = lax.broadcasted_iota(jnp.int32, (high - low, LANES), 0) + low
        shift = LANES if beyond else 0
        masks = [
            band == jnp.bitwise_and(lane + shift + off_row(k, t, beyond), 2 * LANES - 1) for k in range(links)
        ]
        for h in range(hl):
            d_real, d_imag = adm_row(0, 0, h, t, beyond), adm_row(1, 0, h, t, beyond)
            total_real = jnp.zeros(band.shape, jnp.float32)
            total_imag = jnp.zeros(band.shape, jnp.float32)
            for k in range(links):
                l_real, l_imag = adm_row(0, 1 + k, h, t, beyond), adm_row(1, 1 + k, h, t, beyond)
                total_real += jnp.where(masks[k], d_real * l_real - d_imag * l_imag, 0.0)
                total_imag += jnp.where(masks[k], d_real * l_imag + d_imag * l_real, 0.0)
            weights[h, t, low:high, shift : shift + LANES] = total_real.astype(jnp.bfloat16)
            weights[h, t, low:high, shift + 2 * LANES : shift + 3 * LANES] = total_imag.astype(jnp.bfloat16)

    for t in range(tiles):
        fill(t, False, 0, LANES + 16)
        fill(t, False, 2 * LANES - 16, 2 * LANES)
        for h in range(hl):
            weights[h, t, LANES + 16 : 2 * LANES - 16, :] = jnp.zeros((LANES - 32, 4 * LANES), jnp.bfloat16)
            for at in (LANES, 3 * LANES):
                weights[h, t, 16 : LANES - 16, at : at + LANES] = jnp.zeros((LANES - 32, LANES), jnp.bfloat16)

    @pl.when(has_left)
    def _():
        for copy in side_copies(0):
            copy.wait_recv()

    @pl.when(has_right)
    def _():
        for copy in side_copies(1):
            copy.wait_recv()

    for t in range(tiles):
        for low, high in ((LANES - 16, LANES + 16), (2 * LANES - 16, 2 * LANES), (0, 16)):
            fill(t, True, low, high)

    def all_of(ref, count, out, into):
        return remote(ref.at[pl.ds(0, count)], ref.at[pl.ds(0, count)], out, into, me, y)

    across = (((1,), (1,)), ((), ()))
    eye = jnp.where(lax.broadcasted_iota(jnp.int32, (LANES, LANES), 0) == lane, 1.0, 0.0)
    unit = jnp.concatenate([eye, jnp.zeros((LANES, LANES), jnp.float32)], axis=1)
    for t in range(tiles):
        for h in range(hl):
            own = jnp.concatenate(
                [weights[h, t, :, 0:LANES], weights[h, t, :, 2 * LANES : 3 * LANES]], axis=0
            )
            flipped = lax.dot_general(eye.astype(jnp.bfloat16), own, across, preferred_element_type=jnp.float32)
            step = jnp.concatenate([unit + flipped[:, : 2 * LANES], flipped[:, 2 * LANES :]], axis=0)
            step = step.astype(jnp.bfloat16)
            by_real = lax.dot_general(
                step, weights[h, t, :, 0 : 2 * LANES], across, preferred_element_type=jnp.float32
            )
            by_imag = lax.dot_general(
                step, weights[h, t, :, 2 * LANES :], across, preferred_element_type=jnp.float32
            )
            real = unit + by_real[:LANES] - by_imag[LANES:]
            imag = by_imag[:LANES] + by_real[LANES:]
            d_real = jnp.concatenate([adm_row(0, 0, h, t, False), adm_row(0, 0, h, t, True)], axis=1)
            d_imag = jnp.concatenate([adm_row(1, 0, h, t, False), adm_row(1, 0, h, t, True)], axis=1)
            resp[h, t, 0:LANES] = (real * d_real - imag * d_imag).astype(jnp.bfloat16)
            resp[h, t, LANES:] = (real * d_imag + imag * d_real).astype(jnp.bfloat16)

    all_of(buses, nh - 1, 0, 0).wait_recv()

    @pl.when(has_left)
    def _():
        bus_copy(0, 0, y, 1, 1).wait_recv()

    @pl.when(has_right)
    def _():
        bus_copy(0, nh + 1, y, 2, 2).wait_recv()

    row = lax.broadcasted_iota(jnp.int32, (rows, LANES), 0)
    is_real = row % 8 < conv
    base = jnp.bitwise_and((row // 8 - 1) * sub, 2 * LANES - 1)
    spread = []
    for t in range(tiles):
        near = buses[around * t : around * (t + 1) + 2].astype(jnp.float32).reshape(rows, LANES)
        at_bus = base + near.astype(jnp.int32)
        hits = [jnp.where(at_bus == lane + shift, 1.0, 0.0) for shift in (0, LANES)]
        spread.append(jnp.concatenate([hit.T for hit in hits], axis=0).astype(jnp.bfloat16))

    off_tiles = [off_side[0].astype(jnp.float32)]
    off_tiles += [off_ref[:, LANES * t : LANES * (t + 1)].astype(jnp.float32) for t in range(tiles)]
    off_tiles.append(off_side[1].astype(jnp.float32))
    for m in range(nh):
        offsets = jnp.zeros((1, LANES), jnp.float32)
        for k in range(links):
            inside = jnp.logical_and(lane >= inner * k, lane < inner * (k + 1))
            offsets = jnp.where(inside, window(off_tiles, LANES + sub * m - REACH, inner * k)[k : k + 1], offsets)
        off_row8[m] = jnp.broadcast_to(offsets, (8, LANES))
    used = lane < inner * links
    in_inner = lax.rem(lane, inner)
    ends = in_inner + off_row8[me][0:1].astype(jnp.int32)
    tall = lax.broadcasted_iota(jnp.int32, (LANES, LANES), 0)
    to_inner = jnp.logical_and(jnp.logical_and(lax.rem(tall, inner) == ends, tall < inner * links), used)
    to_outer = jnp.logical_and(tall == ends + REACH, used)
    hops = jnp.concatenate([jnp.where(to_inner, 1.0, 0.0), jnp.where(to_outer, 1.0, 0.0)], axis=0)
    hops = hops.astype(jnp.bfloat16)
    group = 2 * conv * hl
    near_rows = []
    for j in range(3):
        near = buses[me + j].astype(jnp.float32) + float(sub * (j - 1) + 2 * REACH)
        near_rows += [near] * hl
    if 3 * group < LANES:
        near_rows.append(jnp.full((LANES - 3 * group, LANES), -1.0, jnp.float32))
    hit = jnp.concatenate(near_rows, axis=0).astype(jnp.int32) == lane
    part_one = lax.rem(tall, 8) < conv
    picks = [jnp.where(jnp.logical_and(hit, part_one), 1.0, 0.0)]
    picks.append(jnp.where(jnp.logical_and(hit, jnp.logical_not(part_one)), 1.0, 0.0))
    picks = jnp.concatenate(picks, axis=0).astype(jnp.bfloat16)
    size = 2 * deep * conv
    order = LANES // size
    wanted = tall // size * size + lax.rem(tall, conv) * 2 * deep + lax.rem(tall, size) // conv
    shuffle = jnp.where(wanted == lane, 1.0, 0.0).astype(jnp.bfloat16)

    all_of(parcel_recv, nh - 1, 6, 6).wait_recv()

    @pl.when(jnp.logical_or(send_left, send_right))
    def _():
        all_of(parcel_edge, nh, 11, 11).wait_recv()

    parcel = parcel_recv[...].astype(jnp.float32) + parcel_edge[...].astype(jnp.float32)
    line_all = parcel[:, : 2 * deep]
    self_all = parcel[:, 2 * deep :]
    real_row = lax.broadcasted_iota(jnp.int32, (nh, 2 * deep, LANES), 1) < deep

    def swap(x):
        return pltpu.roll(x, deep, 1)

    def turned(x):
        return jnp.where(real_row, -swap(x), swap(x))

    line_turned, self_turned = turned(line_all), turned(self_all)

    def times(x, y_all, y_turned):
        other = swap(x)
        return jnp.where(real_row, x, other) * y_all + jnp.where(real_row, other, x) * y_turned

    flat, full = (nh * 2 * deep, LANES), (nh, 2 * deep, LANES)
    numbers_own = [bus_ref[c] - first for c in range(conv)]
    begins = []
    for c in range(conv):
        at_line = jnp.logical_and(in_inner == numbers_own[c] + REACH, used)
        begins.append(jnp.where(at_line, line_all.reshape(flat), 0.0).astype(jnp.bfloat16))
    one = lax.dot_general(jnp.concatenate(begins, axis=0), hops, across, preferred_element_type=jnp.float32)
    nexts = []
    for c in range(conv):
        here = one[flat[0] * c : flat[0] * (c + 1), :LANES].reshape(full)
        nexts.append(times(here, line_all, line_turned).reshape(flat).astype(jnp.bfloat16))
    two = lax.dot_general(
        jnp.concatenate(nexts, axis=0), hops[LANES:], across, preferred_element_type=jnp.float32
    )
    rows_at = []
    for c in range(conv):
        cut = slice(flat[0] * c, flat[0] * (c + 1))
        start = jnp.where(jnp.logical_and(real_row, lane == numbers_own[c] + 2 * REACH), 1.0, 0.0)
        reached = start + (one[cut, LANES:] + two[cut]).reshape(full)
        rows_at.append(times(reached, self_all, self_turned).reshape(flat).astype(jnp.bfloat16))
    taken = lax.dot_general(jnp.concatenate(rows_at, axis=0), picks, across, preferred_element_type=jnp.float32)
    harm_row = lax.rem(lax.broadcasted_iota(jnp.int32, full, 1), deep)
    same = harm_row == lax.rem(lane // 8, hl)
    answer = []
    for c in range(conv):
        cut = slice(flat[0] * c, flat[0] * (c + 1))
        whole = taken[cut, :LANES].reshape(full) + turned(taken[cut, LANES:].reshape(full))
        answer.append(jnp.where(same, whole, 0.0).astype(jnp.bfloat16))
    sorted_rows = []
    for b in range(nh // order):
        block_rows = [answer[c][order * b + i] for i in range(order) for c in range(conv)]
        mixed = jnp.dot(shuffle, jnp.concatenate(block_rows, axis=0), preferred_element_type=jnp.float32)
        sorted_rows.append(mixed.astype(jnp.bfloat16))

    all_of(recv, nh - 1, 3, 3).wait_recv()

    @pl.when(has_left)
    def _():
        spec_copy(0, 0, y, 4, 4).wait_recv()

    @pl.when(has_right)
    def _():
        spec_copy(0, nh + 1, y, 5, 5).wait_recv()

    injected, solved, volts_now = [], [], []
    for t in range(tiles):
        parts = []
        for h in range(hl):
            here = recv[around * t : around * (t + 1) + 2, h].astype(jnp.float32).reshape(rows, LANES)
            parts += [jnp.where(is_real, here, 0.0), jnp.where(is_real, 0.0, here)]
        parts = jnp.concatenate(parts, axis=1).astype(jnp.bfloat16)
        injected.append(jnp.dot(spread[t], parts, preferred_element_type=jnp.float32).astype(jnp.bfloat16))
    for t in range(tiles):
        for h in range(hl):
            mine = injected[t][:, 2 * LANES * h : 2 * LANES * (h + 1)]
            solved.append(jnp.dot(resp[h, t], mine, preferred_element_type=jnp.float32))
    for t in range(tiles):
        now = []
        for h in range(hl):
            both = solved[t * hl + h]
            real = both[:LANES, :LANES] - both[LANES:, LANES:]
            imag = both[:LANES, LANES:] + both[LANES:, :LANES]
            now.append(jnp.concatenate([real, imag], axis=0).astype(jnp.bfloat16))
        volts_now.append(now)
    for t in range(tiles):
        for h in range(hl):
            out_ref[:, h, LANES * t : LANES * (t + 1)] = volts_now[t][h].reshape(2, LANES, LANES)

    @pl.when(near_left)
    def _():
        near_copy(0, me, y).wait_recv()

    @pl.when(near_right)
    def _():
        near_copy(1, me, y).wait_recv()

    for source in range(nh):
        around_here = jnp.concatenate(
            [near_spec[0, source].reshape(group, LANES), send[source].reshape(group, LANES)]
            + [near_spec[1, source].reshape(group, LANES)],
            axis=0,
        )
        at = size * (source % order)
        mine = sorted_rows[source // order][at : at + size, : 3 * group]
        at_conv = jnp.dot(mine, around_here, preferred_element_type=jnp.float32)
        at_conv = at_conv.reshape(2, deep, conv, LANES).astype(jnp.bfloat16)
        next_ref[:, hl * source : hl * (source + 1)] = at_conv[:, :hl]

    all_of(buses, nh - 1, 0, 0).wait_send()
    all_of(recv, nh - 1, 3, 3).wait_send()

    @pl.when(has_right)
    def _():
        for copy in side_copies(0):
            copy.wait_send()

    @pl.when(has_left)
    def _():
        for copy in side_copies(1):
            copy.wait_send()

    @pl.when(send_right)
    def _():
        all_of(buses, nh, 1, 1).wait_send()
        all_of(recv, nh, 4, 4).wait_send()

    @pl.when(send_left)
    def _():
        all_of(buses, nh, 2, 2).wait_send()
        all_of(recv, nh, 5, 5).wait_send()

    all_of(parcel_recv, nh - 1, 6, 6).wait_send()

    @pl.when(has_right)
    def _():
        edge_copy(0, me, y).wait_send()

    @pl.when(has_left)
    def _():
        edge_copy(1, me, y).wait_send()

    @pl.when(near_right)
    def _():
        near_copy(0, me, y).wait_send()

    @pl.when(near_left)
    def _():
        near_copy(1, me, y).wait_send()


def store(volt_ref, next_ref, volt_out, next_out, sems):
    copies = [pltpu.make_async_copy(volt_ref.at[p], volt_out.at[p], sems.at[p]) for p in range(2)]
    copies.append(pltpu.make_async_copy(next_ref, next_out, sems.at[2]))
    for copy in copies:
        copy.start()
    for copy in copies:
        copy.wait()


def local(nh, ny, conv_volt, conv_power, conv_type, type_steep, conv_bus, admittance, link_offset):
    _, orders, conv, snaps = conv_volt.shape
    hl = orders // nh
    block = admittance.shape[3]
    tiles = block // LANES
    around = LANES * nh // block
    deep = max(hl, 4)
    span = 2 * orders
    basis = make_basis(orders)
    regrouped = basis.reshape(2, orders, NT).transpose(1, 0, 2).reshape(span, NT)
    vmem = pl.BlockSpec(memory_space=pltpu.VMEM)
    anywhere = pl.BlockSpec(memory_space=pl.ANY)
    bf16 = jnp.bfloat16
    dma = pltpu.SemaphoreType.DMA
    volt_shape, next_shape = (2, hl, block, snaps), (2, orders, conv, snaps)
    solved = pl.pallas_call(
        functools.partial(kernel, nh, ny),
        out_shape=(pltpu.VMEM(volt_shape, bf16), pltpu.VMEM(next_shape, bf16)),
        in_specs=[anywhere] * 9,
        out_specs=(vmem, vmem),
        scratch_shapes=[
            pltpu.VMEM((span * conv, snaps), bf16),
            pltpu.SMEM(conv_type.shape, jnp.int32),
            pltpu.SMEM(type_steep.shape, jnp.float32),
            pltpu.VMEM((conv, snaps), jnp.float32),
            pltpu.SMEM(conv_bus.shape, jnp.int32),
            pltpu.VMEM(admittance.shape, jnp.float32),
            pltpu.VMEM(link_offset.shape, jnp.int32),
            pltpu.VMEM((NT, span), bf16),
            pltpu.VMEM((span, NT), bf16),
            pltpu.VMEM((span * conv + 8, LANES), jnp.float32),
            pltpu.VMEM((span, conv * LANES), bf16),
            pltpu.VMEM((nh, hl, 8, LANES), bf16),
            pltpu.VMEM((nh + 2, hl, 8, LANES), bf16),
            pltpu.VMEM((8, LANES), bf16),
            pltpu.VMEM((nh + 2, 8, LANES), bf16),
            pltpu.VMEM((2,) + admittance.shape[:3] + (LANES,), jnp.float32),
            pltpu.VMEM((2, link_offset.shape[0], LANES), jnp.int32),
            pltpu.VMEM((hl, tiles, 2 * LANES, 4 * LANES), bf16),
            pltpu.VMEM((hl, tiles, 2 * LANES, 2 * LANES), bf16),
            pltpu.VMEM((nh + 2, 4 * deep, LANES), bf16),
            pltpu.VMEM((nh, 4 * deep, LANES), bf16),
            pltpu.VMEM((nh, 4 * deep, LANES), bf16),
            pltpu.VMEM((2, nh, hl, 8, LANES), bf16),
            pltpu.VMEM((nh, 8, LANES), jnp.float32),
            dma((9,)),
            dma((15,)),
            dma((15,)),
        ],
        compiler_params=pltpu.CompilerParams(collective_id=0, has_side_effects=True, vmem_limit_bytes=56 * 2**20),
        name="power_flow",
    )(
        conv_volt.reshape(span * conv, snaps),
        conv_power,
        conv_type,
        type_steep,
        conv_bus,
        admittance,
        link_offset,
        jnp.asarray(basis.T, bf16),
        jnp.asarray(regrouped, bf16),
    )
    return pl.pallas_call(
        store,
        out_shape=(jax.ShapeDtypeStruct(volt_shape, bf16), jax.ShapeDtypeStruct(next_shape, bf16)),
        in_specs=[vmem, vmem],
        out_specs=(anywhere, anywhere),
        scratch_shapes=[dma((3,))],
        compiler_params=pltpu.CompilerParams(vmem_limit_bytes=32 * 2**20),
        name="store_results",
    )(*solved)


def solution(mesh):
    in_specs = (
        P(None, None, ("bus", "harm"), None),
        P(("bus", "harm"), None),
        P(("bus", "harm")),
        P(),
        P(("bus", "harm")),
        P(None, None, "harm", "bus"),
        P(None, "bus"),
    )
    out_specs = (P(None, "harm", "bus", None), P(None, None, ("bus", "harm"), None))
    body = functools.partial(local, mesh.shape["harm"], mesh.shape["bus"])
    return jax.shard_map(body, mesh=mesh, in_specs=in_specs, out_specs=out_specs, check_vma=False)
```

```python
import functools
import math

import jax
import jax.numpy as jnp
import numpy as np
from jax import lax
from jax.experimental import pallas as pl
from jax.experimental.pallas import tpu as pltpu
from jax.sharding import PartitionSpec as P

NT = 1024
LANES = 128
REACH = 8
CHUNKS = 4


def make_basis(orders):
    samples = np.arange(NT)
    phases = (np.arange(1, orders + 1)[:, None] * samples[None, :] % NT) * (2.0 * math.pi / NT)
    return np.concatenate([np.cos(phases), -np.sin(phases)], axis=0).astype(np.float32)


def kernel(
    nh,
    ny,
    volt_hbm,
    power_hbm,
    type_hbm,
    steep_hbm,
    bus_hbm,
    adm_hbm,
    off_hbm,
    fwd_hbm,
    inv_hbm,
    out_ref,
    next_ref,
    volt_ref,
    type_ref,
    steep_ref,
    power_ref,
    bus_ref,
    adm_ref,
    off_ref,
    fwd_ref,
    inv_ref,
    wide,
    volts,
    send,
    recv,
    my_bus,
    buses,
    adm_side,
    off_side,
    weights,
    resp,
    parcels,
    parcel_recv,
    parcel_edge,
    near_spec,
    off_row8,
    load_sem,
    send_sem,
    recv_sem,
):
    me = lax.axis_index("harm")
    y = lax.axis_index("bus")
    hl = adm_ref.shape[2]
    block = adm_ref.shape[3]
    links = off_ref.shape[0]
    conv = power_ref.shape[0]
    sub = block // nh
    tiles = block // LANES
    around = LANES // sub
    rows = 8 * (around + 2)
    deep = parcels.shape[1] // 3
    inner, outer = sub + 2 * REACH, sub + 4 * REACH
    has_left = y > 0
    has_right = y < ny - 1
    place = y * nh + me
    near_left, near_right = place > 0, place < ny * nh - 1
    send_right = jnp.logical_and(has_right, me == nh - 1)
    send_left = jnp.logical_and(has_left, me == 0)

    pairs = (
        (volt_hbm, volt_ref),
        (fwd_hbm, fwd_ref),
        (type_hbm, type_ref),
        (steep_hbm, steep_ref),
        (power_hbm, power_ref),
        (inv_hbm, inv_ref),
        (bus_hbm, bus_ref),
        (adm_hbm, adm_ref),
        (off_hbm, off_ref),
    )
    loads = [pltpu.make_async_copy(src, dst, load_sem.at[i]) for i, (src, dst) in enumerate(pairs)]
    for load in loads:
        load.start()

    barrier = pltpu.get_barrier_semaphore()

    def greet(d, by):
        pl.semaphore_signal(barrier, inc=1, device_id={"harm": d, "bus": by})

    def each(low, body):
        def step(i, carry):
            body(i)
            return carry

        lax.fori_loop(low, nh, step, 0)

    def peer(s):
        return lax.rem(me + s, nh)

    each(1, lambda s: greet(peer(s), y))

    @pl.when(has_left)
    def _():
        each(0, lambda d: greet(d, y - 1))

    @pl.when(has_right)
    def _():
        each(0, lambda d: greet(d, y + 1))

    @pl.when(jnp.logical_not(has_left))
    def _():
        recv[0] = jnp.zeros(recv.shape[1:], recv.dtype)
        buses[0] = jnp.zeros(buses.shape[1:], buses.dtype)
        adm_side[0] = jnp.zeros(adm_side.shape[1:], adm_side.dtype)
        off_side[0] = jnp.zeros(off_side.shape[1:], off_side.dtype)

    @pl.when(jnp.logical_not(has_right))
    def _():
        recv[nh + 1] = jnp.zeros(recv.shape[1:], recv.dtype)
        buses[nh + 1] = jnp.zeros(buses.shape[1:], buses.dtype)
        adm_side[1] = jnp.zeros(adm_side.shape[1:], adm_side.dtype)
        off_side[1] = jnp.zeros(off_side.shape[1:], off_side.dtype)

    @pl.when(jnp.logical_not(jnp.logical_or(send_left, send_right)))
    def _():
        parcel_edge[...] = jnp.zeros(parcel_edge.shape, parcel_edge.dtype)

    @pl.when(jnp.logical_not(near_left))
    def _():
        near_spec[0] = jnp.zeros(near_spec.shape[1:], near_spec.dtype)

    @pl.when(jnp.logical_not(near_right))
    def _():
        near_spec[1] = jnp.zeros(near_spec.shape[1:], near_spec.dtype)

    loads[0].wait()
    span = volt_ref.shape[0] // conv
    wide[0 : span * conv] = volt_ref[...].astype(jnp.float32)
    for c in range(conv):
        volts[:, LANES * c : LANES * (c + 1)] = wide[pl.ds(c, span, stride=conv), :].astype(jnp.bfloat16)

    for load in loads[1:5]:
        load.wait()

    def steepness(c):
        value = steep_ref[0]
        for kind in range(1, steep_ref.shape[0]):
            value = jnp.where(type_ref[c] == kind, steep_ref[kind], value)
        return jnp.full((1, LANES), value, jnp.float32)

    steep = jnp.concatenate([steepness(c) for c in range(conv)], axis=1)
    power = jnp.concatenate([power_ref[c : c + 1, :] for c in range(conv)], axis=1) * NT ** (-0.5)
    loads[5].wait()
    part = NT // CHUNKS
    spectra = jnp.zeros((span, conv * LANES), jnp.float32)
    for q in range(CHUNKS):
        wave = jnp.dot(fwd_ref[part * q : part * (q + 1), :], volts[...], preferred_element_type=jnp.float32)
        now = jnp.tanh(steep * wave).astype(jnp.bfloat16)
        spectra = spectra + jnp.dot(
            inv_ref[:, part * q : part * (q + 1)], now, preferred_element_type=jnp.float32
        )
    spectra = spectra * power
    for c in range(conv):
        wide[pl.ds(c, span, stride=conv), :] = spectra[:, LANES * c : LANES * (c + 1)]
    send[...] = wide[0 : span * conv].reshape(nh, hl, 8, LANES).astype(jnp.bfloat16)

    for load in loads[6:]:
        load.wait()
    first = (y * nh + me) * sub
    row8 = lax.broadcasted_iota(jnp.int32, (8, LANES), 0) % conv
    numbers = jnp.zeros((8, LANES), jnp.float32)
    for c in range(conv):
        numbers = jnp.where(row8 == c, (bus_ref[c] - first).astype(jnp.float32), numbers)
    my_bus[...] = numbers.astype(jnp.bfloat16)

    lane = lax.broadcasted_iota(jnp.int32, (1, LANES), 1)

    def window(pieces, start, at):
        first_piece = start // LANES
        shift = (at - start) % LANES
        moved = []
        for piece in (first_piece, first_piece + 1):
            if 0 <= piece < len(pieces):
                moved.append(pltpu.roll(pieces[piece], shift, 1) if shift else pieces[piece])
            else:
                moved.append(jnp.zeros(pieces[0].shape, pieces[0].dtype))
        return jnp.where(lane - at < LANES * (first_piece + 1) - start, moved[0], moved[1])

    def stacked(real, imag):
        if deep == hl:
            return jnp.concatenate([real, imag], axis=0)
        empty = jnp.zeros((deep - hl, LANES), jnp.float32)
        return jnp.concatenate([real, empty, imag, empty], axis=0)

    selfs, lines = [[], []], [[] for _ in range(links)]
    for t in range(tiles):
        cut = slice(LANES * t, LANES * (t + 1))
        d_real, d_imag = adm_ref[0, 0, :, cut], adm_ref[1, 0, :, cut]
        for p, value in enumerate((d_real, d_imag)):
            if deep > hl:
                value = jnp.concatenate([value, jnp.zeros((deep - hl, LANES), jnp.float32)], axis=0)
            selfs[p].append(value)
        for k in range(links):
            l_real, l_imag = adm_ref[0, 1 + k, :, cut], adm_ref[1, 1 + k, :, cut]
            lines[k].append(stacked(d_real * l_real - d_imag * l_imag, d_real * l_imag + d_imag * l_real))
    for m in range(-1, nh + 1):
        line_part = numbers if 2 * deep == 8 else jnp.concatenate([numbers] * (deep // 4), axis=0)
        for k in range(links):
            inside = jnp.logical_and(lane >= inner * k, lane < inner * (k + 1))
            line_part = jnp.where(inside, window(lines[k], sub * m - REACH, inner * k), line_part)
        self_parts = [window(selfs[p], sub * m - 2 * REACH, outer * p) for p in range(2)]
        self_part = jnp.where(lane < outer, self_parts[0], jnp.where(lane < 2 * outer, self_parts[1], 0.0))
        parcels[m + 1] = jnp.concatenate([line_part, self_part], axis=0).astype(jnp.bfloat16)

    pl.semaphore_wait(barrier, nh - 1 + nh * has_left.astype(jnp.int32) + nh * has_right.astype(jnp.int32))

    def remote(src, dst, out, into, d, by):
        return pltpu.make_async_remote_copy(
            src_ref=src,
            dst_ref=dst,
            send_sem=send_sem.at[out],
            recv_sem=recv_sem.at[into],
            device_id={"harm": d, "bus": by},
        )

    def bus_copy(d, slot, by, out, into):
        return remote(my_bus, buses.at[slot], out, into, d, by)

    def spec_copy(d, slot, by, out, into):
        return remote(send.at[d], recv.at[slot], out, into, d, by)

    def parcel_copy(d):
        return remote(parcels.at[d + 1], parcel_recv.at[me], 6, 6, d, y)

    def edge_copy(side, d, by):
        own_parcel = parcels.at[nh + 1 if side == 0 else 0]
        return remote(own_parcel, parcel_edge.at[me], 11 + side, 11, d, by)

    def near_copy(side, d, by):
        return remote(send, near_spec.at[side], 13 + side, 13 + side, d, by)

    up, down = lax.rem(y + 1, ny), lax.rem(y + ny - 1, ny)

    def side_copies(side):
        by = y + 1 if side == 0 else y - 1
        start = block - LANES if side == 0 else 0
        return (
            remote(adm_ref.at[:, :, :, pl.ds(start, LANES)], adm_side.at[side], 7 + side, 7 + side, me, by),
            remote(off_ref.at[:, pl.ds(start, LANES)], off_side.at[side], 9 + side, 9 + side, me, by),
        )

    @pl.when(has_right)
    def _():
        for copy in side_copies(0):
            copy.start()

    @pl.when(has_left)
    def _():
        for copy in side_copies(1):
            copy.start()

    @pl.when(send_right)
    def _():
        each(0, lambda d: bus_copy(d, 0, y + 1, 1, 1).start())
        each(0, lambda d: spec_copy(d, 0, y + 1, 4, 4).start())

    @pl.when(send_left)
    def _():
        each(0, lambda d: bus_copy(d, nh + 1, y - 1, 2, 2).start())
        each(0, lambda d: spec_copy(d, nh + 1, y - 1, 5, 5).start())

    for s in range(1, nh):
        parcel_copy(peer(s)).start()

    @pl.when(has_right)
    def _():
        edge_copy(0, lax.rem(me + nh - me, nh), up).start()

    @pl.when(has_left)
    def _():
        edge_copy(1, lax.rem(me + 2 * nh - 1 - me, nh), down).start()

    for s in range(1, nh):
        spec_copy(peer(s), me + 1, y, 3, 3).start()

    recv[me + 1] = send[me]
    parcel_recv[me] = parcels[me + 1]

    is_right = lane < LANES // 2

    def adm_row(p, k, h, t, beyond):
        def row_of(t):
            if t < 0:
                return adm_side[0, p, k, h : h + 1, :]
            if t >= tiles:
                return adm_side[1, p, k, h : h + 1, :]
            return adm_ref[p, k, h : h + 1, LANES * t : LANES * (t + 1)]

        return jnp.where(is_right, row_of(t + 1), row_of(t - 1)) if beyond else row_of(t)

    def off_row(k, t, beyond):
        def row_of(t):
            if t < 0:
                return off_side[0, k : k + 1, :]
            if t >= tiles:
                return off_side[1, k : k + 1, :]
            return off_ref[k : k + 1, LANES * t : LANES * (t + 1)]

        return jnp.where(is_right, row_of(t + 1), row_of(t - 1)) if beyond else row_of(t)

    def fill(t, beyond, low, high):
        band = lax.broadcasted_iota(jnp.int32, (high - low, LANES), 0) + low
        shift = LANES if beyond else 0
        masks = [
            band == jnp.bitwise_and(lane + shift + off_row(k, t, beyond), 2 * LANES - 1) for k in range(links)
        ]
        for h in range(hl):
            d_real, d_imag = adm_row(0, 0, h, t, beyond), adm_row(1, 0, h, t, beyond)
            total_real = jnp.zeros(band.shape, jnp.float32)
            total_imag = jnp.zeros(band.shape, jnp.float32)
            for k in range(links):
                l_real, l_imag = adm_row(0, 1 + k, h, t, beyond), adm_row(1, 1 + k, h, t, beyond)
                total_real += jnp.where(masks[k], d_real * l_real - d_imag * l_imag, 0.0)
                total_imag += jnp.where(masks[k], d_real * l_imag + d_imag * l_real, 0.0)
            weights[h, t, low:high, shift : shift + LANES] = total_real.astype(jnp.bfloat16)
            weights[h, t, low:high, shift + 2 * LANES : shift + 3 * LANES] = total_imag.astype(jnp.bfloat16)

    for t in range(tiles):
        fill(t, False, 0, LANES + 16)
        fill(t, False, 2 * LANES - 16, 2 * LANES)
        for h in range(hl):
            weights[h, t, LANES + 16 : 2 * LANES - 16, :] = jnp.zeros((LANES - 32, 4 * LANES), jnp.bfloat16)
            for at in (LANES, 3 * LANES):
                weights[h, t, 16 : LANES - 16, at : at + LANES] = jnp.zeros((LANES - 32, LANES), jnp.bfloat16)

    @pl.when(me < nh - 1)
    def _():
        near_copy(0, peer(1), y).start()

    @pl.when(me > 0)
    def _():
        near_copy(1, peer(nh - 1), y).start()

    @pl.when(send_right)
    def _():
        near_copy(0, peer(1), up).start()

    @pl.when(send_left)
    def _():
        near_copy(1, peer(nh - 1), down).start()

    @pl.when(has_left)
    def _():
        for copy in side_copies(0):
            copy.wait_recv()

    @pl.when(has_right)
    def _():
        for copy in side_copies(1):
            copy.wait_recv()

    for t in range(tiles):
        for low, high in ((LANES - 16, LANES + 16), (2 * LANES - 16, 2 * LANES), (0, 16)):
            fill(t, True, low, high)

    def all_of(ref, count, out, into):
        return remote(ref.at[pl.ds(0, count)], ref.at[pl.ds(0, count)], out, into, me, y)

    across = (((1,), (1,)), ((), ()))
    eye = jnp.where(lax.broadcasted_iota(jnp.int32, (LANES, LANES), 0) == lane, 1.0, 0.0)
    unit = jnp.concatenate([eye, jnp.zeros((LANES, LANES), jnp.float32)], axis=1)
    for t in range(tiles):
        for h in range(hl):
            own = jnp.concatenate(
                [weights[h, t, :, 0:LANES], weights[h, t, :, 2 * LANES : 3 * LANES]], axis=0
            )
            flipped = lax.dot_general(eye.astype(jnp.bfloat16), own, across, preferred_element_type=jnp.float32)
            step = jnp.concatenate([unit + flipped[:, : 2 * LANES], flipped[:, 2 * LANES :]], axis=0)
            step = step.astype(jnp.bfloat16)
            by_real = lax.dot_general(
                step, weights[h, t, :, 0 : 2 * LANES], across, preferred_element_type=jnp.float32
            )
            by_imag = lax.dot_general(
                step, weights[h, t, :, 2 * LANES :], across, preferred_element_type=jnp.float32
            )
            real = unit + by_real[:LANES] - by_imag[LANES:]
            imag = by_imag[:LANES] + by_real[LANES:]
            d_real = jnp.concatenate([adm_row(0, 0, h, t, False), adm_row(0, 0, h, t, True)], axis=1)
            d_imag = jnp.concatenate([adm_row(1, 0, h, t, False), adm_row(1, 0, h, t, True)], axis=1)
            resp[h, t, 0:LANES] = (real * d_real - imag * d_imag).astype(jnp.bfloat16)
            resp[h, t, LANES:] = (real * d_imag + imag * d_real).astype(jnp.bfloat16)

    all_of(parcel_recv, nh - 1, 6, 6).wait_recv()
    given = parcel_recv[...].astype(jnp.float32)
    buses[1 : nh + 1] = jnp.broadcast_to(given[:, :8, LANES - 1 :], (nh, 8, LANES)).astype(jnp.bfloat16)

    off_tiles = [off_side[0].astype(jnp.float32)]
    off_tiles += [off_ref[:, LANES * t : LANES * (t + 1)].astype(jnp.float32) for t in range(tiles)]
    off_tiles.append(off_side[1].astype(jnp.float32))
    for m in range(nh):
        offsets = jnp.zeros((1, LANES), jnp.float32)
        for k in range(links):
            inside = jnp.logical_and(lane >= inner * k, lane < inner * (k + 1))
            offsets = jnp.where(inside, window(off_tiles, LANES + sub * m - REACH, inner * k)[k : k + 1], offsets)
        off_row8[m] = jnp.broadcast_to(offsets, (8, LANES))
    used = lane < inner * links
    in_inner = lax.rem(lane, inner)
    ends = in_inner + off_row8[me][0:1].astype(jnp.int32)
    tall = lax.broadcasted_iota(jnp.int32, (LANES, LANES), 0)
    to_inner = jnp.logical_and(jnp.logical_and(lax.rem(tall, inner) == ends, tall < inner * links), used)
    to_outer = jnp.logical_and(tall == ends + REACH, used)
    hops = jnp.concatenate([jnp.where(to_inner, 1.0, 0.0), jnp.where(to_outer, 1.0, 0.0)], axis=0)
    hops = hops.astype(jnp.bfloat16)
    size = 2 * deep * conv
    order = LANES // size
    wanted = tall // size * size + lax.rem(tall, conv) * 2 * deep + lax.rem(tall, size) // conv
    shuffle = jnp.where(wanted == lane, 1.0, 0.0).astype(jnp.bfloat16)

    @pl.when(jnp.logical_or(send_left, send_right))
    def _():
        all_of(parcel_edge, nh, 11, 11).wait_recv()

    parcel = given + parcel_edge[...].astype(jnp.float32)
    line_all = parcel[:, : 2 * deep]
    self_both = parcel[:, 2 * deep :]
    self_all = jnp.concatenate([self_both, pltpu.roll(self_both, LANES - outer, 2)], axis=1)
    real_row = lax.broadcasted_iota(jnp.int32, (nh, 2 * deep, LANES), 1) < deep

    def swap(x):
        return pltpu.roll(x, deep, 1)

    def turned(x):
        return jnp.where(real_row, -swap(x), swap(x))

    line_turned, self_turned = turned(line_all), turned(self_all)

    def times(x, y_all, y_turned):
        other = swap(x)
        return jnp.where(real_row, x, other) * y_all + jnp.where(real_row, other, x) * y_turned

    flat, full = (nh * 2 * deep, LANES), (nh, 2 * deep, LANES)
    numbers_own = [bus_ref[c] - first for c in range(conv)]
    begins = []
    for c in range(conv):
        at_line = jnp.logical_and(in_inner == numbers_own[c] + REACH, used)
        begins.append(jnp.where(at_line, line_all.reshape(flat), 0.0).astype(jnp.bfloat16))
    one = lax.dot_general(jnp.concatenate(begins, axis=0), hops, across, preferred_element_type=jnp.float32)
    nexts = []
    for c in range(conv):
        here = one[flat[0] * c : flat[0] * (c + 1), :LANES].reshape(full)
        nexts.append(times(here, line_all, line_turned).reshape(flat).astype(jnp.bfloat16))
    two = lax.dot_general(
        jnp.concatenate(nexts, axis=0), hops[LANES:], across, preferred_element_type=jnp.float32
    )
    rows_at = []
    for c in range(conv):
        cut = slice(flat[0] * c, flat[0] * (c + 1))
        start = jnp.where(jnp.logical_and(real_row, lane == numbers_own[c] + 2 * REACH), 1.0, 0.0)
        reached = start + (one[cut, LANES:] + two[cut]).reshape(full)
        rows_at.append(times(reached, self_all, self_turned).reshape(flat).astype(jnp.bfloat16))
    @pl.when(has_left)
    def _():
        bus_copy(0, 0, y, 1, 1).wait_recv()

    @pl.when(has_right)
    def _():
        bus_copy(0, nh + 1, y, 2, 2).wait_recv()

    group = 2 * conv * hl
    near_rows = []
    for j in range(3):
        near = buses[me + j].astype(jnp.float32) + float(sub * (j - 1) + 2 * REACH)
        near_rows += [near] * hl
    if 3 * group < LANES:
        near_rows.append(jnp.full((LANES - 3 * group, LANES), -1.0, jnp.float32))
    hit = jnp.concatenate(near_rows, axis=0).astype(jnp.int32) == lane
    part_one = lax.rem(tall, 8) < conv
    picks = [jnp.where(jnp.logical_and(hit, part_one), 1.0, 0.0)]
    picks.append(jnp.where(jnp.logical_and(hit, jnp.logical_not(part_one)), 1.0, 0.0))
    picks = jnp.concatenate(picks, axis=0).astype(jnp.bfloat16)
    taken = lax.dot_general(jnp.concatenate(rows_at, axis=0), picks, across, preferred_element_type=jnp.float32)
    harm_row = lax.rem(lax.broadcasted_iota(jnp.int32, full, 1), deep)
    same = harm_row == lax.rem(lane // 8, hl)
    answer = []
    for c in range(conv):
        cut = slice(flat[0] * c, flat[0] * (c + 1))
        whole = taken[cut, :LANES].reshape(full) + turned(taken[cut, LANES:].reshape(full))
        answer.append(jnp.where(same, whole, 0.0).astype(jnp.bfloat16))
    sorted_rows = []
    for b in range(nh // order):
        block_rows = [answer[c][order * b + i] for i in range(order) for c in range(conv)]
        mixed = jnp.dot(shuffle, jnp.concatenate(block_rows, axis=0), preferred_element_type=jnp.float32)
        sorted_rows.append(mixed.astype(jnp.bfloat16))

    row = lax.broadcasted_iota(jnp.int32, (rows, LANES), 0)
    is_real = row % 8 < conv
    base = jnp.bitwise_and((row // 8 - 1) * sub, 2 * LANES - 1)
    spread = []
    for t in range(tiles):
        near = buses[around * t : around * (t + 1) + 2].astype(jnp.float32).reshape(rows, LANES)
        at_bus = base + near.astype(jnp.int32)
        hits = [jnp.where(at_bus == lane + shift, 1.0, 0.0) for shift in (0, LANES)]
        spread.append(jnp.concatenate([hit.T for hit in hits], axis=0).astype(jnp.bfloat16))


    all_of(recv, nh - 1, 3, 3).wait_recv()

    @pl.when(has_left)
    def _():
        spec_copy(0, 0, y, 4, 4).wait_recv()

    @pl.when(has_right)
    def _():
        spec_copy(0, nh + 1, y, 5, 5).wait_recv()

    injected, solved, volts_now = [], [], []
    for t in range(tiles):
        parts = []
        for h in range(hl):
            here = recv[around * t : around * (t + 1) + 2, h].astype(jnp.float32).reshape(rows, LANES)
            parts += [jnp.where(is_real, here, 0.0), jnp.where(is_real, 0.0, here)]
        parts = jnp.concatenate(parts, axis=1).astype(jnp.bfloat16)
        injected.append(jnp.dot(spread[t], parts, preferred_element_type=jnp.float32).astype(jnp.bfloat16))
    for t in range(tiles):
        for h in range(hl):
            mine = injected[t][:, 2 * LANES * h : 2 * LANES * (h + 1)]
            solved.append(jnp.dot(resp[h, t], mine, preferred_element_type=jnp.float32))
    for t in range(tiles):
        now = []
        for h in range(hl):
            both = solved[t * hl + h]
            real = both[:LANES, :LANES] - both[LANES:, LANES:]
            imag = both[:LANES, LANES:] + both[LANES:, :LANES]
            now.append(jnp.concatenate([real, imag], axis=0).astype(jnp.bfloat16))
        volts_now.append(now)
    for t in range(tiles):
        for h in range(hl):
            out_ref[:, h, LANES * t : LANES * (t + 1)] = volts_now[t][h].reshape(2, LANES, LANES)

    @pl.when(near_left)
    def _():
        near_copy(0, me, y).wait_recv()

    @pl.when(near_right)
    def _():
        near_copy(1, me, y).wait_recv()

    for source in range(nh):
        around_here = jnp.concatenate(
            [near_spec[0, source].reshape(group, LANES), send[source].reshape(group, LANES)]
            + [near_spec[1, source].reshape(group, LANES)],
            axis=0,
        )
        at = size * (source % order)
        mine = sorted_rows[source // order][at : at + size, : 3 * group]
        at_conv = jnp.dot(mine, around_here, preferred_element_type=jnp.float32)
        at_conv = at_conv.reshape(2, deep, conv, LANES).astype(jnp.bfloat16)
        next_ref[:, hl * source : hl * (source + 1)] = at_conv[:, :hl]

    all_of(recv, nh - 1, 3, 3).wait_send()

    @pl.when(has_right)
    def _():
        for copy in side_copies(0):
            copy.wait_send()

    @pl.when(has_left)
    def _():
        for copy in side_copies(1):
            copy.wait_send()

    @pl.when(send_right)
    def _():
        all_of(buses, nh, 1, 1).wait_send()
        all_of(recv, nh, 4, 4).wait_send()

    @pl.when(send_left)
    def _():
        all_of(buses, nh, 2, 2).wait_send()
        all_of(recv, nh, 5, 5).wait_send()

    all_of(parcel_recv, nh - 1, 6, 6).wait_send()

    @pl.when(has_right)
    def _():
        edge_copy(0, me, y).wait_send()

    @pl.when(has_left)
    def _():
        edge_copy(1, me, y).wait_send()

    @pl.when(near_right)
    def _():
        near_copy(0, me, y).wait_send()

    @pl.when(near_left)
    def _():
        near_copy(1, me, y).wait_send()


def store(volt_ref, next_ref, volt_out, next_out, sems):
    copies = [pltpu.make_async_copy(volt_ref.at[p], volt_out.at[p], sems.at[p]) for p in range(2)]
    copies.append(pltpu.make_async_copy(next_ref, next_out, sems.at[2]))
    for copy in copies:
        copy.start()
    for copy in copies:
        copy.wait()


def local(nh, ny, conv_volt, conv_power, conv_type, type_steep, conv_bus, admittance, link_offset):
    _, orders, conv, snaps = conv_volt.shape
    hl = orders // nh
    block = admittance.shape[3]
    tiles = block // LANES
    around = LANES * nh // block
    deep = max(hl, 4)
    span = 2 * orders
    basis = make_basis(orders)
    regrouped = basis.reshape(2, orders, NT).transpose(1, 0, 2).reshape(span, NT)
    vmem = pl.BlockSpec(memory_space=pltpu.VMEM)
    anywhere = pl.BlockSpec(memory_space=pl.ANY)
    bf16 = jnp.bfloat16
    dma = pltpu.SemaphoreType.DMA
    volt_shape, next_shape = (2, hl, block, snaps), (2, orders, conv, snaps)
    solved = pl.pallas_call(
        functools.partial(kernel, nh, ny),
        out_shape=(pltpu.VMEM(volt_shape, bf16), pltpu.VMEM(next_shape, bf16)),
        in_specs=[anywhere] * 9,
        out_specs=(vmem, vmem),
        scratch_shapes=[
            pltpu.VMEM((span * conv, snaps), bf16),
            pltpu.SMEM(conv_type.shape, jnp.int32),
            pltpu.SMEM(type_steep.shape, jnp.float32),
            pltpu.VMEM((conv, snaps), jnp.float32),
            pltpu.SMEM(conv_bus.shape, jnp.int32),
            pltpu.VMEM(admittance.shape, jnp.float32),
            pltpu.VMEM(link_offset.shape, jnp.int32),
            pltpu.VMEM((NT, span), bf16),
            pltpu.VMEM((span, NT), bf16),
            pltpu.VMEM((span * conv + 8, LANES), jnp.float32),
            pltpu.VMEM((span, conv * LANES), bf16),
            pltpu.VMEM((nh, hl, 8, LANES), bf16),
            pltpu.VMEM((nh + 2, hl, 8, LANES), bf16),
            pltpu.VMEM((8, LANES), bf16),
            pltpu.VMEM((nh + 2, 8, LANES), bf16),
            pltpu.VMEM((2,) + admittance.shape[:3] + (LANES,), jnp.float32),
            pltpu.VMEM((2, link_offset.shape[0], LANES), jnp.int32),
            pltpu.VMEM((hl, tiles, 2 * LANES, 4 * LANES), bf16),
            pltpu.VMEM((hl, tiles, 2 * LANES, 2 * LANES), bf16),
            pltpu.VMEM((nh + 2, 3 * deep, LANES), bf16),
            pltpu.VMEM((nh, 3 * deep, LANES), bf16),
            pltpu.VMEM((nh, 3 * deep, LANES), bf16),
            pltpu.VMEM((2, nh, hl, 8, LANES), bf16),
            pltpu.VMEM((nh, 8, LANES), jnp.float32),
            dma((9,)),
            dma((15,)),
            dma((15,)),
        ],
        compiler_params=pltpu.CompilerParams(collective_id=0, has_side_effects=True, vmem_limit_bytes=56 * 2**20),
        name="power_flow",
    )(
        conv_volt.reshape(span * conv, snaps),
        conv_power,
        conv_type,
        type_steep,
        conv_bus,
        admittance,
        link_offset,
        jnp.asarray(basis.T, bf16),
        jnp.asarray(regrouped, bf16),
    )
    return pl.pallas_call(
        store,
        out_shape=(jax.ShapeDtypeStruct(volt_shape, bf16), jax.ShapeDtypeStruct(next_shape, bf16)),
        in_specs=[vmem, vmem],
        out_specs=(anywhere, anywhere),
        scratch_shapes=[dma((3,))],
        compiler_params=pltpu.CompilerParams(vmem_limit_bytes=32 * 2**20),
        name="store_results",
    )(*solved)


def solution(mesh):
    in_specs = (
        P(None, None, ("bus", "harm"), None),
        P(("bus", "harm"), None),
        P(("bus", "harm")),
        P(),
        P(("bus", "harm")),
        P(None, None, "harm", "bus"),
        P(None, "bus"),
    )
    out_specs = (P(None, "harm", "bus", None), P(None, None, ("bus", "harm"), None))
    body = functools.partial(local, mesh.shape["harm"], mesh.shape["bus"])
    return jax.shard_map(body, mesh=mesh, in_specs=in_specs, out_specs=out_specs, check_vma=False)
```

```python
import functools
import math

import jax
import jax.numpy as jnp
import numpy as np
from jax import lax
from jax.experimental import pallas as pl
from jax.experimental.pallas import tpu as pltpu
from jax.sharding import PartitionSpec as P

NT = 1024
LANES = 128
REACH = 8
CHUNKS = 4


def make_basis(orders):
    samples = np.arange(NT)
    phases = (np.arange(1, orders + 1)[:, None] * samples[None, :] % NT) * (2.0 * math.pi / NT)
    return np.concatenate([np.cos(phases), -np.sin(phases)], axis=0).astype(np.float32)


def kernel(
    nh,
    ny,
    volt_hbm,
    power_hbm,
    type_hbm,
    steep_hbm,
    bus_hbm,
    adm_hbm,
    off_hbm,
    fwd_hbm,
    inv_hbm,
    out_ref,
    next_ref,
    volt_ref,
    type_ref,
    steep_ref,
    power_ref,
    bus_ref,
    adm_ref,
    off_ref,
    fwd_ref,
    inv_ref,
    wide,
    volts,
    send,
    recv,
    my_bus,
    buses,
    adm_side,
    off_side,
    weights,
    resp,
    parcels,
    parcel_recv,
    parcel_edge,
    near_spec,
    off_row8,
    load_sem,
    send_sem,
    recv_sem,
):
    me = lax.axis_index("harm")
    y = lax.axis_index("bus")
    hl = adm_ref.shape[2]
    block = adm_ref.shape[3]
    links = off_ref.shape[0]
    conv = power_ref.shape[0]
    sub = block // nh
    tiles = block // LANES
    around = LANES // sub
    rows = 8 * (around + 2)
    deep = parcels.shape[1] // 3
    inner, outer = sub + 2 * REACH, sub + 4 * REACH
    has_left = y > 0
    has_right = y < ny - 1
    place = y * nh + me
    near_left, near_right = place > 0, place < ny * nh - 1
    send_right = jnp.logical_and(has_right, me == nh - 1)
    send_left = jnp.logical_and(has_left, me == 0)

    pairs = (
        (bus_hbm, bus_ref),
        (adm_hbm, adm_ref),
        (off_hbm, off_ref),
        (volt_hbm, volt_ref),
        (fwd_hbm, fwd_ref),
        (type_hbm, type_ref),
        (steep_hbm, steep_ref),
        (power_hbm, power_ref),
        (inv_hbm, inv_ref),
    )
    loads = [pltpu.make_async_copy(src, dst, load_sem.at[i]) for i, (src, dst) in enumerate(pairs)]
    for load in loads:
        load.start()

    barrier = pltpu.get_barrier_semaphore()

    def greet(d, by):
        pl.semaphore_signal(barrier, inc=1, device_id={"harm": d, "bus": by})

    def each(low, body):
        def step(i, carry):
            body(i)
            return carry

        lax.fori_loop(low, nh, step, 0)

    def peer(s):
        return lax.rem(me + s, nh)

    each(1, lambda s: greet(peer(s), y))

    @pl.when(has_left)
    def _():
        each(0, lambda d: greet(d, y - 1))

    @pl.when(has_right)
    def _():
        each(0, lambda d: greet(d, y + 1))

    @pl.when(jnp.logical_not(has_left))
    def _():
        recv[0] = jnp.zeros(recv.shape[1:], recv.dtype)
        buses[0] = jnp.zeros(buses.shape[1:], buses.dtype)
        adm_side[0] = jnp.zeros(adm_side.shape[1:], adm_side.dtype)
        off_side[0] = jnp.zeros(off_side.shape[1:], off_side.dtype)

    @pl.when(jnp.logical_not(has_right))
    def _():
        recv[nh + 1] = jnp.zeros(recv.shape[1:], recv.dtype)
        buses[nh + 1] = jnp.zeros(buses.shape[1:], buses.dtype)
        adm_side[1] = jnp.zeros(adm_side.shape[1:], adm_side.dtype)
        off_side[1] = jnp.zeros(off_side.shape[1:], off_side.dtype)

    @pl.when(jnp.logical_not(jnp.logical_or(send_left, send_right)))
    def _():
        parcel_edge[...] = jnp.zeros(parcel_edge.shape, parcel_edge.dtype)

    @pl.when(jnp.logical_not(near_left))
    def _():
        near_spec[0] = jnp.zeros(near_spec.shape[1:], near_spec.dtype)

    @pl.when(jnp.logical_not(near_right))
    def _():
        near_spec[1] = jnp.zeros(near_spec.shape[1:], near_spec.dtype)

    for load in loads[:3]:
        load.wait()
    first = (y * nh + me) * sub
    row8 = lax.broadcasted_iota(jnp.int32, (8, LANES), 0) % conv
    numbers = jnp.zeros((8, LANES), jnp.float32)
    for c in range(conv):
        numbers = jnp.where(row8 == c, (bus_ref[c] - first).astype(jnp.float32), numbers)
    my_bus[...] = numbers.astype(jnp.bfloat16)

    lane = lax.broadcasted_iota(jnp.int32, (1, LANES), 1)

    def window(pieces, start, at):
        first_piece = start // LANES
        shift = (at - start) % LANES
        moved = []
        for piece in (first_piece, first_piece + 1):
            if 0 <= piece < len(pieces):
                moved.append(pltpu.roll(pieces[piece], shift, 1) if shift else pieces[piece])
            else:
                moved.append(jnp.zeros(pieces[0].shape, pieces[0].dtype))
        return jnp.where(lane - at < LANES * (first_piece + 1) - start, moved[0], moved[1])

    def stacked(real, imag):
        if deep == hl:
            return jnp.concatenate([real, imag], axis=0)
        empty = jnp.zeros((deep - hl, LANES), jnp.float32)
        return jnp.concatenate([real, empty, imag, empty], axis=0)

    selfs, lines = [[], []], [[] for _ in range(links)]
    for t in range(tiles):
        cut = slice(LANES * t, LANES * (t + 1))
        d_real, d_imag = adm_ref[0, 0, :, cut], adm_ref[1, 0, :, cut]
        for p, value in enumerate((d_real, d_imag)):
            if deep > hl:
                value = jnp.concatenate([value, jnp.zeros((deep - hl, LANES), jnp.float32)], axis=0)
            selfs[p].append(value)
        for k in range(links):
            l_real, l_imag = adm_ref[0, 1 + k, :, cut], adm_ref[1, 1 + k, :, cut]
            lines[k].append(stacked(d_real * l_real - d_imag * l_imag, d_real * l_imag + d_imag * l_real))
    for m in range(-1, nh + 1):
        line_part = numbers if 2 * deep == 8 else jnp.concatenate([numbers] * (deep // 4), axis=0)
        for k in range(links):
            inside = jnp.logical_and(lane >= inner * k, lane < inner * (k + 1))
            line_part = jnp.where(inside, window(lines[k], sub * m - REACH, inner * k), line_part)
        self_parts = [window(selfs[p], sub * m - 2 * REACH, outer * p) for p in range(2)]
        self_part = jnp.where(lane < outer, self_parts[0], jnp.where(lane < 2 * outer, self_parts[1], 0.0))
        parcels[m + 1] = jnp.concatenate([line_part, self_part], axis=0).astype(jnp.bfloat16)

    loads[3].wait()
    span = volt_ref.shape[0] // conv
    wide[0 : span * conv] = volt_ref[...].astype(jnp.float32)
    for c in range(conv):
        volts[:, LANES * c : LANES * (c + 1)] = wide[pl.ds(c, span, stride=conv), :].astype(jnp.bfloat16)

    for load in loads[4:8]:
        load.wait()

    def steepness(c):
        value = steep_ref[0]
        for kind in range(1, steep_ref.shape[0]):
            value = jnp.where(type_ref[c] == kind, steep_ref[kind], value)
        return jnp.full((1, LANES), value, jnp.float32)

    steep = jnp.concatenate([steepness(c) for c in range(conv)], axis=1)
    power = jnp.concatenate([power_ref[c : c + 1, :] for c in range(conv)], axis=1) * NT ** (-0.5)
    loads[8].wait()
    part = NT // CHUNKS
    spectra = jnp.zeros((span, conv * LANES), jnp.float32)
    for q in range(CHUNKS):
        wave = jnp.dot(fwd_ref[part * q : part * (q + 1), :], volts[...], preferred_element_type=jnp.float32)
        now = jnp.tanh(steep * wave).astype(jnp.bfloat16)
        spectra = spectra + jnp.dot(
            inv_ref[:, part * q : part * (q + 1)], now, preferred_element_type=jnp.float32
        )
    spectra = spectra * power
    for c in range(conv):
        wide[pl.ds(c, span, stride=conv), :] = spectra[:, LANES * c : LANES * (c + 1)]
    send[...] = wide[0 : span * conv].reshape(nh, hl, 8, LANES).astype(jnp.bfloat16)

    pl.semaphore_wait(barrier, nh - 1 + nh * has_left.astype(jnp.int32) + nh * has_right.astype(jnp.int32))

    def remote(src, dst, out, into, d, by):
        return pltpu.make_async_remote_copy(
            src_ref=src,
            dst_ref=dst,
            send_sem=send_sem.at[out],
            recv_sem=recv_sem.at[into],
            device_id={"harm": d, "bus": by},
        )

    def bus_copy(d, slot, by, out, into):
        return remote(my_bus, buses.at[slot], out, into, d, by)

    def spec_copy(d, slot, by, out, into):
        return remote(send.at[d], recv.at[slot], out, into, d, by)

    def parcel_copy(d):
        return remote(parcels.at[d + 1], parcel_recv.at[me], 6, 6, d, y)

    def edge_copy(side, d, by):
        own_parcel = parcels.at[nh + 1 if side == 0 else 0]
        return remote(own_parcel, parcel_edge.at[me], 11 + side, 11, d, by)

    def near_copy(side, d, by):
        return remote(send, near_spec.at[side], 13 + side, 13 + side, d, by)

    up, down = lax.rem(y + 1, ny), lax.rem(y + ny - 1, ny)

    def side_copies(side):
        by = y + 1 if side == 0 else y - 1
        start = block - LANES if side == 0 else 0
        return (
            remote(adm_ref.at[:, :, :, pl.ds(start, LANES)], adm_side.at[side], 7 + side, 7 + side, me, by),
            remote(off_ref.at[:, pl.ds(start, LANES)], off_side.at[side], 9 + side, 9 + side, me, by),
        )

    @pl.when(has_right)
    def _():
        for copy in side_copies(0):
            copy.start()

    @pl.when(has_left)
    def _():
        for copy in side_copies(1):
            copy.start()

    @pl.when(send_right)
    def _():
        each(0, lambda d: bus_copy(d, 0, y + 1, 1, 1).start())
        each(0, lambda d: spec_copy(d, 0, y + 1, 4, 4).start())

    @pl.when(send_left)
    def _():
        each(0, lambda d: bus_copy(d, nh + 1, y - 1, 2, 2).start())
        each(0, lambda d: spec_copy(d, nh + 1, y - 1, 5, 5).start())

    for s in range(1, nh):
        parcel_copy(peer(s)).start()

    @pl.when(has_right)
    def _():
        edge_copy(0, lax.rem(me + nh - me, nh), up).start()

    @pl.when(has_left)
    def _():
        edge_copy(1, lax.rem(me + 2 * nh - 1 - me, nh), down).start()

    for s in range(1, nh):
        spec_copy(peer(s), me + 1, y, 3, 3).start()

    recv[me + 1] = send[me]
    parcel_recv[me] = parcels[me + 1]

    is_right = lane < LANES // 2

    def adm_row(p, k, h, t, beyond):
        def row_of(t):
            if t < 0:
                return adm_side[0, p, k, h : h + 1, :]
            if t >= tiles:
                return adm_side[1, p, k, h : h + 1, :]
            return adm_ref[p, k, h : h + 1, LANES * t : LANES * (t + 1)]

        return jnp.where(is_right, row_of(t + 1), row_of(t - 1)) if beyond else row_of(t)

    def off_row(k, t, beyond):
        def row_of(t):
            if t < 0:
                return off_side[0, k : k + 1, :]
            if t >= tiles:
                return off_side[1, k : k + 1, :]
            return off_ref[k : k + 1, LANES * t : LANES * (t + 1)]

        return jnp.where(is_right, row_of(t + 1), row_of(t - 1)) if beyond else row_of(t)

    def fill(t, beyond, low, high):
        band = lax.broadcasted_iota(jnp.int32, (high - low, LANES), 0) + low
        shift = LANES if beyond else 0
        masks = [
            band == jnp.bitwise_and(lane + shift + off_row(k, t, beyond), 2 * LANES - 1) for k in range(links)
        ]
        for h in range(hl):
            d_real, d_imag = adm_row(0, 0, h, t, beyond), adm_row(1, 0, h, t, beyond)
            total_real = jnp.zeros(band.shape, jnp.float32)
            total_imag = jnp.zeros(band.shape, jnp.float32)
            for k in range(links):
                l_real, l_imag = adm_row(0, 1 + k, h, t, beyond), adm_row(1, 1 + k, h, t, beyond)
                total_real += jnp.where(masks[k], d_real * l_real - d_imag * l_imag, 0.0)
                total_imag += jnp.where(masks[k], d_real * l_imag + d_imag * l_real, 0.0)
            weights[h, t, low:high, shift : shift + LANES] = total_real.astype(jnp.bfloat16)
            weights[h, t, low:high, shift + 2 * LANES : shift + 3 * LANES] = total_imag.astype(jnp.bfloat16)

    for t in range(tiles):
        fill(t, False, 0, LANES + 16)
        fill(t, False, 2 * LANES - 16, 2 * LANES)
        for h in range(hl):
            weights[h, t, LANES + 16 : 2 * LANES - 16, :] = jnp.zeros((LANES - 32, 4 * LANES), jnp.bfloat16)
            for at in (LANES, 3 * LANES):
                weights[h, t, 16 : LANES - 16, at : at + LANES] = jnp.zeros((LANES - 32, LANES), jnp.bfloat16)

    @pl.when(me < nh - 1)
    def _():
        near_copy(0, peer(1), y).start()

    @pl.when(me > 0)
    def _():
        near_copy(1, peer(nh - 1), y).start()

    @pl.when(send_right)
    def _():
        near_copy(0, peer(1), up).start()

    @pl.when(send_left)
    def _():
        near_copy(1, peer(nh - 1), down).start()

    @pl.when(has_left)
    def _():
        for copy in side_copies(0):
            copy.wait_recv()

    @pl.when(has_right)
    def _():
        for copy in side_copies(1):
            copy.wait_recv()

    for t in range(tiles):
        for low, high in ((LANES - 16, LANES + 16), (2 * LANES - 16, 2 * LANES), (0, 16)):
            fill(t, True, low, high)

    def all_of(ref, count, out, into):
        return remote(ref.at[pl.ds(0, count)], ref.at[pl.ds(0, count)], out, into, me, y)

    across = (((1,), (1,)), ((), ()))
    eye = jnp.where(lax.broadcasted_iota(jnp.int32, (LANES, LANES), 0) == lane, 1.0, 0.0)
    unit = jnp.concatenate([eye, jnp.zeros((LANES, LANES), jnp.float32)], axis=1)
    for t in range(tiles):
        for h in range(hl):
            own = jnp.concatenate(
                [weights[h, t, :, 0:LANES], weights[h, t, :, 2 * LANES : 3 * LANES]], axis=0
            )
            flipped = lax.dot_general(eye.astype(jnp.bfloat16), own, across, preferred_element_type=jnp.float32)
            step = jnp.concatenate([unit + flipped[:, : 2 * LANES], flipped[:, 2 * LANES :]], axis=0)
            step = step.astype(jnp.bfloat16)
            by_real = lax.dot_general(
                step, weights[h, t, :, 0 : 2 * LANES], across, preferred_element_type=jnp.float32
            )
            by_imag = lax.dot_general(
                step, weights[h, t, :, 2 * LANES :], across, preferred_element_type=jnp.float32
            )
            real = unit + by_real[:LANES] - by_imag[LANES:]
            imag = by_imag[:LANES] + by_real[LANES:]
            d_real = jnp.concatenate([adm_row(0, 0, h, t, False), adm_row(0, 0, h, t, True)], axis=1)
            d_imag = jnp.concatenate([adm_row(1, 0, h, t, False), adm_row(1, 0, h, t, True)], axis=1)
            resp[h, t, 0:LANES] = (real * d_real - imag * d_imag).astype(jnp.bfloat16)
            resp[h, t, LANES:] = (real * d_imag + imag * d_real).astype(jnp.bfloat16)

    all_of(parcel_recv, nh - 1, 6, 6).wait_recv()
    given = parcel_recv[...].astype(jnp.float32)
    buses[1 : nh + 1] = jnp.broadcast_to(given[:, :8, LANES - 1 :], (nh, 8, LANES)).astype(jnp.bfloat16)

    off_tiles = [off_side[0].astype(jnp.float32)]
    off_tiles += [off_ref[:, LANES * t : LANES * (t + 1)].astype(jnp.float32) for t in range(tiles)]
    off_tiles.append(off_side[1].astype(jnp.float32))
    for m in range(nh):
        offsets = jnp.zeros((1, LANES), jnp.float32)
        for k in range(links):
            inside = jnp.logical_and(lane >= inner * k, lane < inner * (k + 1))
            offsets = jnp.where(inside, window(off_tiles, LANES + sub * m - REACH, inner * k)[k : k + 1], offsets)
        off_row8[m] = jnp.broadcast_to(offsets, (8, LANES))
    used = lane < inner * links
    in_inner = lax.rem(lane, inner)
    ends = in_inner + off_row8[me][0:1].astype(jnp.int32)
    tall = lax.broadcasted_iota(jnp.int32, (LANES, LANES), 0)
    to_inner = jnp.logical_and(jnp.logical_and(lax.rem(tall, inner) == ends, tall < inner * links), used)
    to_outer = jnp.logical_and(tall == ends + REACH, used)
    hops = jnp.concatenate([jnp.where(to_inner, 1.0, 0.0), jnp.where(to_outer, 1.0, 0.0)], axis=0)
    hops = hops.astype(jnp.bfloat16)
    size = 2 * deep * conv
    order = LANES // size
    wanted = tall // size * size + lax.rem(tall, conv) * 2 * deep + lax.rem(tall, size) // conv
    shuffle = jnp.where(wanted == lane, 1.0, 0.0).astype(jnp.bfloat16)

    @pl.when(jnp.logical_or(send_left, send_right))
    def _():
        all_of(parcel_edge, nh, 11, 11).wait_recv()

    parcel = given + parcel_edge[...].astype(jnp.float32)
    line_all = parcel[:, : 2 * deep]
    self_both = parcel[:, 2 * deep :]
    self_all = jnp.concatenate([self_both, pltpu.roll(self_both, LANES - outer, 2)], axis=1)
    real_row = lax.broadcasted_iota(jnp.int32, (nh, 2 * deep, LANES), 1) < deep

    def swap(x):
        return pltpu.roll(x, deep, 1)

    def turned(x):
        return jnp.where(real_row, -swap(x), swap(x))

    line_turned, self_turned = turned(line_all), turned(self_all)

    def times(x, y_all, y_turned):
        other = swap(x)
        return jnp.where(real_row, x, other) * y_all + jnp.where(real_row, other, x) * y_turned

    flat, full = (nh * 2 * deep, LANES), (nh, 2 * deep, LANES)
    numbers_own = [bus_ref[c] - first for c in range(conv)]
    begins = []
    for c in range(conv):
        at_line = jnp.logical_and(in_inner == numbers_own[c] + REACH, used)
        begins.append(jnp.where(at_line, line_all.reshape(flat), 0.0).astype(jnp.bfloat16))
    one = lax.dot_general(jnp.concatenate(begins, axis=0), hops, across, preferred_element_type=jnp.float32)
    nexts = []
    for c in range(conv):
        here = one[flat[0] * c : flat[0] * (c + 1), :LANES].reshape(full)
        nexts.append(times(here, line_all, line_turned).reshape(flat).astype(jnp.bfloat16))
    two = lax.dot_general(
        jnp.concatenate(nexts, axis=0), hops[LANES:], across, preferred_element_type=jnp.float32
    )
    rows_at = []
    for c in range(conv):
        cut = slice(flat[0] * c, flat[0] * (c + 1))
        start = jnp.where(jnp.logical_and(real_row, lane == numbers_own[c] + 2 * REACH), 1.0, 0.0)
        reached = start + (one[cut, LANES:] + two[cut]).reshape(full)
        rows_at.append(times(reached, self_all, self_turned).reshape(flat).astype(jnp.bfloat16))
    @pl.when(has_left)
    def _():
        bus_copy(0, 0, y, 1, 1).wait_recv()

    @pl.when(has_right)
    def _():
        bus_copy(0, nh + 1, y, 2, 2).wait_recv()

    group = 2 * conv * hl
    near_rows = []
    for j in range(3):
        near = buses[me + j].astype(jnp.float32) + float(sub * (j - 1) + 2 * REACH)
        near_rows += [near] * hl
    if 3 * group < LANES:
        near_rows.append(jnp.full((LANES - 3 * group, LANES), -1.0, jnp.float32))
    hit = jnp.concatenate(near_rows, axis=0).astype(jnp.int32) == lane
    part_one = lax.rem(tall, 8) < conv
    picks = [jnp.where(jnp.logical_and(hit, part_one), 1.0, 0.0)]
    picks.append(jnp.where(jnp.logical_and(hit, jnp.logical_not(part_one)), 1.0, 0.0))
    picks = jnp.concatenate(picks, axis=0).astype(jnp.bfloat16)
    taken = lax.dot_general(jnp.concatenate(rows_at, axis=0), picks, across, preferred_element_type=jnp.float32)
    harm_row = lax.rem(lax.broadcasted_iota(jnp.int32, full, 1), deep)
    same = harm_row == lax.rem(lane // 8, hl)
    answer = []
    for c in range(conv):
        cut = slice(flat[0] * c, flat[0] * (c + 1))
        whole = taken[cut, :LANES].reshape(full) + turned(taken[cut, LANES:].reshape(full))
        answer.append(jnp.where(same, whole, 0.0).astype(jnp.bfloat16))
    sorted_rows = []
    for b in range(nh // order):
        block_rows = [answer[c][order * b + i] for i in range(order) for c in range(conv)]
        mixed = jnp.dot(shuffle, jnp.concatenate(block_rows, axis=0), preferred_element_type=jnp.float32)
        sorted_rows.append(mixed.astype(jnp.bfloat16))

    row = lax.broadcasted_iota(jnp.int32, (rows, LANES), 0)
    is_real = row % 8 < conv
    base = jnp.bitwise_and((row // 8 - 1) * sub, 2 * LANES - 1)
    spread = []
    for t in range(tiles):
        near = buses[around * t : around * (t + 1) + 2].astype(jnp.float32).reshape(rows, LANES)
        at_bus = base + near.astype(jnp.int32)
        hits = [jnp.where(at_bus == lane + shift, 1.0, 0.0) for shift in (0, LANES)]
        spread.append(jnp.concatenate([hit.T for hit in hits], axis=0).astype(jnp.bfloat16))


    all_of(recv, nh - 1, 3, 3).wait_recv()

    @pl.when(has_left)
    def _():
        spec_copy(0, 0, y, 4, 4).wait_recv()

    @pl.when(has_right)
    def _():
        spec_copy(0, nh + 1, y, 5, 5).wait_recv()

    injected, solved, volts_now = [], [], []
    for t in range(tiles):
        parts = []
        for h in range(hl):
            here = recv[around * t : around * (t + 1) + 2, h].astype(jnp.float32).reshape(rows, LANES)
            parts += [jnp.where(is_real, here, 0.0), jnp.where(is_real, 0.0, here)]
        parts = jnp.concatenate(parts, axis=1).astype(jnp.bfloat16)
        injected.append(jnp.dot(spread[t], parts, preferred_element_type=jnp.float32).astype(jnp.bfloat16))
    for t in range(tiles):
        for h in range(hl):
            mine = injected[t][:, 2 * LANES * h : 2 * LANES * (h + 1)]
            solved.append(jnp.dot(resp[h, t], mine, preferred_element_type=jnp.float32))
    for t in range(tiles):
        now = []
        for h in range(hl):
            both = solved[t * hl + h]
            real = both[:LANES, :LANES] - both[LANES:, LANES:]
            imag = both[:LANES, LANES:] + both[LANES:, :LANES]
            now.append(jnp.concatenate([real, imag], axis=0).astype(jnp.bfloat16))
        volts_now.append(now)
    for t in range(tiles):
        for h in range(hl):
            out_ref[:, h, LANES * t : LANES * (t + 1)] = volts_now[t][h].reshape(2, LANES, LANES)

    @pl.when(near_left)
    def _():
        near_copy(0, me, y).wait_recv()

    @pl.when(near_right)
    def _():
        near_copy(1, me, y).wait_recv()

    for source in range(nh):
        around_here = jnp.concatenate(
            [near_spec[0, source].reshape(group, LANES), send[source].reshape(group, LANES)]
            + [near_spec[1, source].reshape(group, LANES)],
            axis=0,
        )
        at = size * (source % order)
        mine = sorted_rows[source // order][at : at + size, : 3 * group]
        at_conv = jnp.dot(mine, around_here, preferred_element_type=jnp.float32)
        at_conv = at_conv.reshape(2, deep, conv, LANES).astype(jnp.bfloat16)
        next_ref[:, hl * source : hl * (source + 1)] = at_conv[:, :hl]

    all_of(recv, nh - 1, 3, 3).wait_send()

    @pl.when(has_right)
    def _():
        for copy in side_copies(0):
            copy.wait_send()

    @pl.when(has_left)
    def _():
        for copy in side_copies(1):
            copy.wait_send()

    @pl.when(send_right)
    def _():
        all_of(buses, nh, 1, 1).wait_send()
        all_of(recv, nh, 4, 4).wait_send()

    @pl.when(send_left)
    def _():
        all_of(buses, nh, 2, 2).wait_send()
        all_of(recv, nh, 5, 5).wait_send()

    all_of(parcel_recv, nh - 1, 6, 6).wait_send()

    @pl.when(has_right)
    def _():
        edge_copy(0, me, y).wait_send()

    @pl.when(has_left)
    def _():
        edge_copy(1, me, y).wait_send()

    @pl.when(near_right)
    def _():
        near_copy(0, me, y).wait_send()

    @pl.when(near_left)
    def _():
        near_copy(1, me, y).wait_send()


def store(volt_ref, next_ref, volt_out, next_out, sems):
    copies = [pltpu.make_async_copy(volt_ref.at[p], volt_out.at[p], sems.at[p]) for p in range(2)]
    copies.append(pltpu.make_async_copy(next_ref, next_out, sems.at[2]))
    for copy in copies:
        copy.start()
    for copy in copies:
        copy.wait()


def local(nh, ny, conv_volt, conv_power, conv_type, type_steep, conv_bus, admittance, link_offset):
    _, orders, conv, snaps = conv_volt.shape
    hl = orders // nh
    block = admittance.shape[3]
    tiles = block // LANES
    around = LANES * nh // block
    deep = max(hl, 4)
    span = 2 * orders
    basis = make_basis(orders)
    regrouped = basis.reshape(2, orders, NT).transpose(1, 0, 2).reshape(span, NT)
    vmem = pl.BlockSpec(memory_space=pltpu.VMEM)
    anywhere = pl.BlockSpec(memory_space=pl.ANY)
    bf16 = jnp.bfloat16
    dma = pltpu.SemaphoreType.DMA
    volt_shape, next_shape = (2, hl, block, snaps), (2, orders, conv, snaps)
    solved = pl.pallas_call(
        functools.partial(kernel, nh, ny),
        out_shape=(pltpu.VMEM(volt_shape, bf16), pltpu.VMEM(next_shape, bf16)),
        in_specs=[anywhere] * 9,
        out_specs=(vmem, vmem),
        scratch_shapes=[
            pltpu.VMEM((span * conv, snaps), bf16),
            pltpu.SMEM(conv_type.shape, jnp.int32),
            pltpu.SMEM(type_steep.shape, jnp.float32),
            pltpu.VMEM((conv, snaps), jnp.float32),
            pltpu.SMEM(conv_bus.shape, jnp.int32),
            pltpu.VMEM(admittance.shape, jnp.float32),
            pltpu.VMEM(link_offset.shape, jnp.int32),
            pltpu.VMEM((NT, span), bf16),
            pltpu.VMEM((span, NT), bf16),
            pltpu.VMEM((span * conv + 8, LANES), jnp.float32),
            pltpu.VMEM((span, conv * LANES), bf16),
            pltpu.VMEM((nh, hl, 8, LANES), bf16),
            pltpu.VMEM((nh + 2, hl, 8, LANES), bf16),
            pltpu.VMEM((8, LANES), bf16),
            pltpu.VMEM((nh + 2, 8, LANES), bf16),
            pltpu.VMEM((2,) + admittance.shape[:3] + (LANES,), jnp.float32),
            pltpu.VMEM((2, link_offset.shape[0], LANES), jnp.int32),
            pltpu.VMEM((hl, tiles, 2 * LANES, 4 * LANES), bf16),
            pltpu.VMEM((hl, tiles, 2 * LANES, 2 * LANES), bf16),
            pltpu.VMEM((nh + 2, 3 * deep, LANES), bf16),
            pltpu.VMEM((nh, 3 * deep, LANES), bf16),
            pltpu.VMEM((nh, 3 * deep, LANES), bf16),
            pltpu.VMEM((2, nh, hl, 8, LANES), bf16),
            pltpu.VMEM((nh, 8, LANES), jnp.float32),
            dma((9,)),
            dma((15,)),
            dma((15,)),
        ],
        compiler_params=pltpu.CompilerParams(collective_id=0, has_side_effects=True, vmem_limit_bytes=56 * 2**20),
        name="power_flow",
    )(
        conv_volt.reshape(span * conv, snaps),
        conv_power,
        conv_type,
        type_steep,
        conv_bus,
        admittance,
        link_offset,
        jnp.asarray(basis.T, bf16),
        jnp.asarray(regrouped, bf16),
    )
    return pl.pallas_call(
        store,
        out_shape=(jax.ShapeDtypeStruct(volt_shape, bf16), jax.ShapeDtypeStruct(next_shape, bf16)),
        in_specs=[vmem, vmem],
        out_specs=(anywhere, anywhere),
        scratch_shapes=[dma((3,))],
        compiler_params=pltpu.CompilerParams(vmem_limit_bytes=32 * 2**20),
        name="store_results",
    )(*solved)


def solution(mesh):
    in_specs = (
        P(None, None, ("bus", "harm"), None),
        P(("bus", "harm"), None),
        P(("bus", "harm")),
        P(),
        P(("bus", "harm")),
        P(None, None, "harm", "bus"),
        P(None, "bus"),
    )
    out_specs = (P(None, "harm", "bus", None), P(None, None, ("bus", "harm"), None))
    body = functools.partial(local, mesh.shape["harm"], mesh.shape["bus"])
    return jax.shard_map(body, mesh=mesh, in_specs=in_specs, out_specs=out_specs, check_vma=False)
```

```python
import functools
import math

import jax
import jax.numpy as jnp
import numpy as np
from jax import lax
from jax.experimental import pallas as pl
from jax.experimental.pallas import tpu as pltpu
from jax.sharding import PartitionSpec as P

NT = 1024
LANES = 128
REACH = 8
CHUNKS = 4


def make_basis(orders):
    samples = np.arange(NT)
    phases = (np.arange(1, orders + 1)[:, None] * samples[None, :] % NT) * (2.0 * math.pi / NT)
    return np.concatenate([np.cos(phases), -np.sin(phases)], axis=0).astype(np.float32)


def kernel(
    nh,
    ny,
    volt_hbm,
    power_hbm,
    type_hbm,
    steep_hbm,
    bus_hbm,
    adm_hbm,
    off_hbm,
    fwd_hbm,
    inv_hbm,
    out_ref,
    next_ref,
    volt_ref,
    type_ref,
    steep_ref,
    power_ref,
    bus_ref,
    adm_ref,
    off_ref,
    fwd_ref,
    inv_ref,
    wide,
    volts,
    send,
    recv,
    my_bus,
    buses,
    adm_side,
    off_side,
    weights,
    resp,
    parcels,
    parcel_recv,
    parcel_edge,
    near_spec,
    off_row8,
    load_sem,
    send_sem,
    recv_sem,
):
    me = lax.axis_index("harm")
    y = lax.axis_index("bus")
    hl = adm_ref.shape[2]
    block = adm_ref.shape[3]
    links = off_ref.shape[0]
    conv = power_ref.shape[0]
    sub = block // nh
    tiles = block // LANES
    around = LANES // sub
    rows = 8 * (around + 2)
    deep = parcels.shape[1] // 3
    inner, outer = sub + 2 * REACH, sub + 4 * REACH
    has_left = y > 0
    has_right = y < ny - 1
    place = y * nh + me
    near_left, near_right = place > 0, place < ny * nh - 1
    send_right = jnp.logical_and(has_right, me == nh - 1)
    send_left = jnp.logical_and(has_left, me == 0)

    pairs = (
        (bus_hbm, bus_ref),
        (adm_hbm, adm_ref),
        (off_hbm, off_ref),
        (volt_hbm, volt_ref),
        (fwd_hbm, fwd_ref),
        (type_hbm, type_ref),
        (steep_hbm, steep_ref),
        (power_hbm, power_ref),
        (inv_hbm, inv_ref),
    )
    loads = [pltpu.make_async_copy(src, dst, load_sem.at[i]) for i, (src, dst) in enumerate(pairs)]
    for load in loads:
        load.start()

    barrier = pltpu.get_barrier_semaphore()

    def greet(d, by):
        pl.semaphore_signal(barrier, inc=1, device_id={"harm": d, "bus": by})

    def each(low, body):
        def step(i, carry):
            body(i)
            return carry

        lax.fori_loop(low, nh, step, 0)

    def peer(s):
        return lax.rem(me + s, nh)

    each(1, lambda s: greet(peer(s), y))

    @pl.when(has_left)
    def _():
        each(0, lambda d: greet(d, y - 1))

    @pl.when(has_right)
    def _():
        each(0, lambda d: greet(d, y + 1))

    @pl.when(jnp.logical_not(has_left))
    def _():
        recv[0] = jnp.zeros(recv.shape[1:], recv.dtype)
        buses[0] = jnp.zeros(buses.shape[1:], buses.dtype)
        adm_side[0] = jnp.zeros(adm_side.shape[1:], adm_side.dtype)
        off_side[0] = jnp.zeros(off_side.shape[1:], off_side.dtype)

    @pl.when(jnp.logical_not(has_right))
    def _():
        recv[nh + 1] = jnp.zeros(recv.shape[1:], recv.dtype)
        buses[nh + 1] = jnp.zeros(buses.shape[1:], buses.dtype)
        adm_side[1] = jnp.zeros(adm_side.shape[1:], adm_side.dtype)
        off_side[1] = jnp.zeros(off_side.shape[1:], off_side.dtype)

    @pl.when(jnp.logical_not(jnp.logical_or(send_left, send_right)))
    def _():
        parcel_edge[...] = jnp.zeros(parcel_edge.shape, parcel_edge.dtype)

    @pl.when(jnp.logical_not(near_left))
    def _():
        near_spec[0] = jnp.zeros(near_spec.shape[1:], near_spec.dtype)

    @pl.when(jnp.logical_not(near_right))
    def _():
        near_spec[1] = jnp.zeros(near_spec.shape[1:], near_spec.dtype)

    for load in loads[:3]:
        load.wait()
    first = (y * nh + me) * sub
    row8 = lax.broadcasted_iota(jnp.int32, (8, LANES), 0) % conv
    numbers = jnp.zeros((8, LANES), jnp.float32)
    for c in range(conv):
        numbers = jnp.where(row8 == c, (bus_ref[c] - first).astype(jnp.float32), numbers)
    my_bus[...] = numbers.astype(jnp.bfloat16)

    lane = lax.broadcasted_iota(jnp.int32, (1, LANES), 1)

    def window(pieces, start, at):
        first_piece = start // LANES
        shift = (at - start) % LANES
        moved = []
        for piece in (first_piece, first_piece + 1):
            if 0 <= piece < len(pieces):
                moved.append(pltpu.roll(pieces[piece], shift, 1) if shift else pieces[piece])
            else:
                moved.append(jnp.zeros(pieces[0].shape, pieces[0].dtype))
        return jnp.where(lane - at < LANES * (first_piece + 1) - start, moved[0], moved[1])

    def stacked(real, imag):
        if deep == hl:
            return jnp.concatenate([real, imag], axis=0)
        empty = jnp.zeros((deep - hl, LANES), jnp.float32)
        return jnp.concatenate([real, empty, imag, empty], axis=0)

    selfs, lines = [[], []], [[] for _ in range(links)]
    for t in range(tiles):
        cut = slice(LANES * t, LANES * (t + 1))
        d_real, d_imag = adm_ref[0, 0, :, cut], adm_ref[1, 0, :, cut]
        for p, value in enumerate((d_real, d_imag)):
            if deep > hl:
                value = jnp.concatenate([value, jnp.zeros((deep - hl, LANES), jnp.float32)], axis=0)
            selfs[p].append(value)
        for k in range(links):
            l_real, l_imag = adm_ref[0, 1 + k, :, cut], adm_ref[1, 1 + k, :, cut]
            lines[k].append(stacked(d_real * l_real - d_imag * l_imag, d_real * l_imag + d_imag * l_real))
    for m in range(-1, nh + 1):
        line_part = numbers if 2 * deep == 8 else jnp.concatenate([numbers] * (deep // 4), axis=0)
        for k in range(links):
            inside = jnp.logical_and(lane >= inner * k, lane < inner * (k + 1))
            line_part = jnp.where(inside, window(lines[k], sub * m - REACH, inner * k), line_part)
        self_parts = [window(selfs[p], sub * m - 2 * REACH, outer * p) for p in range(2)]
        self_part = jnp.where(lane < outer, self_parts[0], jnp.where(lane < 2 * outer, self_parts[1], 0.0))
        parcels[m + 1] = jnp.concatenate([line_part, self_part], axis=0).astype(jnp.bfloat16)

    loads[3].wait()
    span = volt_ref.shape[0] // conv
    wide[0 : span * conv] = volt_ref[...].astype(jnp.float32)
    for c in range(conv):
        volts[:, LANES * c : LANES * (c + 1)] = wide[pl.ds(c, span, stride=conv), :].astype(jnp.bfloat16)

    for load in loads[4:8]:
        load.wait()

    def steepness(c):
        value = steep_ref[0]
        for kind in range(1, steep_ref.shape[0]):
            value = jnp.where(type_ref[c] == kind, steep_ref[kind], value)
        return jnp.full((1, LANES), value, jnp.float32)

    steep = jnp.concatenate([steepness(c) for c in range(conv)], axis=1)
    power = jnp.concatenate([power_ref[c : c + 1, :] for c in range(conv)], axis=1) * NT ** (-0.5)
    loads[8].wait()
    part = NT // CHUNKS
    spectra = jnp.zeros((span, conv * LANES), jnp.float32)
    for q in range(CHUNKS):
        wave = jnp.dot(fwd_ref[part * q : part * (q + 1), :], volts[...], preferred_element_type=jnp.float32)
        now = jnp.tanh(steep * wave).astype(jnp.bfloat16)
        spectra = spectra + jnp.dot(
            inv_ref[:, part * q : part * (q + 1)], now, preferred_element_type=jnp.float32
        )
    spectra = spectra * power
    for c in range(conv):
        wide[pl.ds(c, span, stride=conv), :] = spectra[:, LANES * c : LANES * (c + 1)]
    send[...] = wide[0 : span * conv].reshape(nh, hl, 8, LANES).astype(jnp.bfloat16)

    pl.semaphore_wait(barrier, nh - 1 + nh * has_left.astype(jnp.int32) + nh * has_right.astype(jnp.int32))

    def remote(src, dst, out, into, d, by):
        return pltpu.make_async_remote_copy(
            src_ref=src,
            dst_ref=dst,
            send_sem=send_sem.at[out],
            recv_sem=recv_sem.at[into],
            device_id={"harm": d, "bus": by},
        )

    def bus_copy(d, slot, by, out, into):
        return remote(my_bus, buses.at[slot], out, into, d, by)

    def spec_copy(d, slot, by, out, into):
        return remote(send.at[d], recv.at[slot], out, into, d, by)

    def parcel_copy(d):
        return remote(parcels.at[d + 1], parcel_recv.at[me], 6, 6, d, y)

    def edge_copy(side, d, by):
        own_parcel = parcels.at[nh + 1 if side == 0 else 0]
        return remote(own_parcel, parcel_edge.at[me], 11 + side, 11, d, by)

    def near_copy(side, d, by):
        return remote(send, near_spec.at[side], 13 + side, 13 + side, d, by)

    up, down = lax.rem(y + 1, ny), lax.rem(y + ny - 1, ny)

    def side_copies(side):
        by = y + 1 if side == 0 else y - 1
        start = block - LANES if side == 0 else 0
        return (
            remote(adm_ref.at[:, :, :, pl.ds(start, LANES)], adm_side.at[side], 7 + side, 7 + side, me, by),
            remote(off_ref.at[:, pl.ds(start, LANES)], off_side.at[side], 9 + side, 9 + side, me, by),
        )

    @pl.when(has_right)
    def _():
        for copy in side_copies(0):
            copy.start()

    @pl.when(has_left)
    def _():
        for copy in side_copies(1):
            copy.start()

    @pl.when(send_right)
    def _():
        each(0, lambda d: bus_copy(d, 0, y + 1, 1, 1).start())
        each(0, lambda d: spec_copy(d, 0, y + 1, 4, 4).start())

    @pl.when(send_left)
    def _():
        each(0, lambda d: bus_copy(d, nh + 1, y - 1, 2, 2).start())
        each(0, lambda d: spec_copy(d, nh + 1, y - 1, 5, 5).start())

    for s in range(1, nh):
        parcel_copy(peer(s)).start()

    @pl.when(has_right)
    def _():
        edge_copy(0, lax.rem(me + nh - me, nh), up).start()

    @pl.when(has_left)
    def _():
        edge_copy(1, lax.rem(me + 2 * nh - 1 - me, nh), down).start()

    for s in range(1, nh):
        spec_copy(peer(s), me + 1, y, 3, 3).start()

    recv[me + 1] = send[me]
    parcel_recv[me] = parcels[me + 1]

    is_right = lane < LANES // 2

    def adm_row(p, k, h, t, beyond):
        def row_of(t):
            if t < 0:
                return adm_side[0, p, k, h : h + 1, :]
            if t >= tiles:
                return adm_side[1, p, k, h : h + 1, :]
            return adm_ref[p, k, h : h + 1, LANES * t : LANES * (t + 1)]

        return jnp.where(is_right, row_of(t + 1), row_of(t - 1)) if beyond else row_of(t)

    def off_row(k, t, beyond):
        def row_of(t):
            if t < 0:
                return off_side[0, k : k + 1, :]
            if t >= tiles:
                return off_side[1, k : k + 1, :]
            return off_ref[k : k + 1, LANES * t : LANES * (t + 1)]

        return jnp.where(is_right, row_of(t + 1), row_of(t - 1)) if beyond else row_of(t)

    def fill(t, beyond, low, high):
        band = lax.broadcasted_iota(jnp.int32, (high - low, LANES), 0) + low
        shift = LANES if beyond else 0
        masks = [
            band == jnp.bitwise_and(lane + shift + off_row(k, t, beyond), 2 * LANES - 1) for k in range(links)
        ]
        for h in range(hl):
            d_real, d_imag = adm_row(0, 0, h, t, beyond), adm_row(1, 0, h, t, beyond)
            total_real = jnp.zeros(band.shape, jnp.float32)
            total_imag = jnp.zeros(band.shape, jnp.float32)
            for k in range(links):
                l_real, l_imag = adm_row(0, 1 + k, h, t, beyond), adm_row(1, 1 + k, h, t, beyond)
                total_real += jnp.where(masks[k], d_real * l_real - d_imag * l_imag, 0.0)
                total_imag += jnp.where(masks[k], d_real * l_imag + d_imag * l_real, 0.0)
            weights[h, t, low:high, shift : shift + LANES] = total_real.astype(jnp.bfloat16)
            weights[h, t, low:high, shift + 2 * LANES : shift + 3 * LANES] = total_imag.astype(jnp.bfloat16)

    for t in range(tiles):
        fill(t, False, 0, LANES + 16)
        fill(t, False, 2 * LANES - 16, 2 * LANES)
        for h in range(hl):
            weights[h, t, LANES + 16 : 2 * LANES - 16, :] = jnp.zeros((LANES - 32, 4 * LANES), jnp.bfloat16)
            for at in (LANES, 3 * LANES):
                weights[h, t, 16 : LANES - 16, at : at + LANES] = jnp.zeros((LANES - 32, LANES), jnp.bfloat16)

    @pl.when(me < nh - 1)
    def _():
        near_copy(0, peer(1), y).start()

    @pl.when(me > 0)
    def _():
        near_copy(1, peer(nh - 1), y).start()

    @pl.when(send_right)
    def _():
        near_copy(0, peer(1), up).start()

    @pl.when(send_left)
    def _():
        near_copy(1, peer(nh - 1), down).start()

    @pl.when(has_left)
    def _():
        for copy in side_copies(0):
            copy.wait_recv()

    @pl.when(has_right)
    def _():
        for copy in side_copies(1):
            copy.wait_recv()

    for t in range(tiles):
        for low, high in ((LANES - 16, LANES + 16), (2 * LANES - 16, 2 * LANES), (0, 16)):
            fill(t, True, low, high)

    def all_of(ref, count, out, into):
        return remote(ref.at[pl.ds(0, count)], ref.at[pl.ds(0, count)], out, into, me, y)

    across = (((1,), (1,)), ((), ()))
    eye = jnp.where(lax.broadcasted_iota(jnp.int32, (LANES, LANES), 0) == lane, 1.0, 0.0)
    unit = jnp.concatenate([eye, jnp.zeros((LANES, LANES), jnp.float32)], axis=1)
    for t in range(tiles):
        for h in range(hl):
            own = jnp.concatenate(
                [weights[h, t, :, 0:LANES], weights[h, t, :, 2 * LANES : 3 * LANES]], axis=0
            )
            flipped = lax.dot_general(eye.astype(jnp.bfloat16), own, across, preferred_element_type=jnp.float32)
            step = jnp.concatenate([unit + flipped[:, : 2 * LANES], flipped[:, 2 * LANES :]], axis=0)
            step = step.astype(jnp.bfloat16)
            by_real = lax.dot_general(
                step, weights[h, t, :, 0 : 2 * LANES], across, preferred_element_type=jnp.float32
            )
            by_imag = lax.dot_general(
                step, weights[h, t, :, 2 * LANES :], across, preferred_element_type=jnp.float32
            )
            real = unit + by_real[:LANES] - by_imag[LANES:]
            imag = by_imag[:LANES] + by_real[LANES:]
            d_real = jnp.concatenate([adm_row(0, 0, h, t, False), adm_row(0, 0, h, t, True)], axis=1)
            d_imag = jnp.concatenate([adm_row(1, 0, h, t, False), adm_row(1, 0, h, t, True)], axis=1)
            resp[h, t, 0:LANES] = (real * d_real - imag * d_imag).astype(jnp.bfloat16)
            resp[h, t, LANES:] = (real * d_imag + imag * d_real).astype(jnp.bfloat16)

    all_of(parcel_recv, nh - 1, 6, 6).wait_recv()
    given = parcel_recv[...].astype(jnp.float32)
    buses[1 : nh + 1] = jnp.broadcast_to(given[:, :8, LANES - 1 :], (nh, 8, LANES)).astype(jnp.bfloat16)

    off_tiles = [off_side[0].astype(jnp.float32)]
    off_tiles += [off_ref[:, LANES * t : LANES * (t + 1)].astype(jnp.float32) for t in range(tiles)]
    off_tiles.append(off_side[1].astype(jnp.float32))
    for m in range(nh):
        offsets = jnp.zeros((1, LANES), jnp.float32)
        for k in range(links):
            inside = jnp.logical_and(lane >= inner * k, lane < inner * (k + 1))
            offsets = jnp.where(inside, window(off_tiles, LANES + sub * m - REACH, inner * k)[k : k + 1], offsets)
        off_row8[m] = jnp.broadcast_to(offsets, (8, LANES))
    used = lane < inner * links
    in_inner = lax.rem(lane, inner)
    ends = in_inner + off_row8[me][0:1].astype(jnp.int32)
    tall = lax.broadcasted_iota(jnp.int32, (LANES, LANES), 0)
    to_inner = jnp.logical_and(jnp.logical_and(lax.rem(tall, inner) == ends, tall < inner * links), used)
    to_outer = jnp.logical_and(tall == ends + REACH, used)
    hops = jnp.concatenate([jnp.where(to_inner, 1.0, 0.0), jnp.where(to_outer, 1.0, 0.0)], axis=0)
    hops = hops.astype(jnp.bfloat16)
    size = 2 * deep * conv
    order = LANES // size
    wanted = tall // size * size + lax.rem(tall, conv) * 2 * deep + lax.rem(tall, size) // conv
    shuffle = jnp.where(wanted == lane, 1.0, 0.0).astype(jnp.bfloat16)

    @pl.when(jnp.logical_or(send_left, send_right))
    def _():
        all_of(parcel_edge, nh, 11, 11).wait_recv()

    parcel = given + parcel_edge[...].astype(jnp.float32)
    line_all = parcel[:, : 2 * deep]
    self_both = parcel[:, 2 * deep :]
    self_all = jnp.concatenate([self_both, pltpu.roll(self_both, LANES - outer, 2)], axis=1)
    real_row = lax.broadcasted_iota(jnp.int32, (nh, 2 * deep, LANES), 1) < deep

    def swap(x):
        return pltpu.roll(x, deep, 1)

    def turned(x):
        return jnp.where(real_row, -swap(x), swap(x))

    line_turned, self_turned = turned(line_all), turned(self_all)

    def times(x, y_all, y_turned):
        other = swap(x)
        return jnp.where(real_row, x, other) * y_all + jnp.where(real_row, other, x) * y_turned

    flat, full = (nh * 2 * deep, LANES), (nh, 2 * deep, LANES)
    numbers_own = [bus_ref[c] - first for c in range(conv)]
    begins = []
    for c in range(conv):
        at_line = jnp.logical_and(in_inner == numbers_own[c] + REACH, used)
        begins.append(jnp.where(at_line, line_all.reshape(flat), 0.0).astype(jnp.bfloat16))
    one = lax.dot_general(jnp.concatenate(begins, axis=0), hops, across, preferred_element_type=jnp.float32)
    nexts = []
    for c in range(conv):
        here = one[flat[0] * c : flat[0] * (c + 1), :LANES].reshape(full)
        nexts.append(times(here, line_all, line_turned).reshape(flat).astype(jnp.bfloat16))
    two = lax.dot_general(
        jnp.concatenate(nexts, axis=0), hops[LANES:], across, preferred_element_type=jnp.float32
    )
    rows_at = []
    for c in range(conv):
        cut = slice(flat[0] * c, flat[0] * (c + 1))
        start = jnp.where(jnp.logical_and(real_row, lane == numbers_own[c] + 2 * REACH), 1.0, 0.0)
        reached = start + (one[cut, LANES:] + two[cut]).reshape(full)
        rows_at.append(times(reached, self_all, self_turned).reshape(flat).astype(jnp.bfloat16))
    @pl.when(has_left)
    def _():
        bus_copy(0, 0, y, 1, 1).wait_recv()

    @pl.when(has_right)
    def _():
        bus_copy(0, nh + 1, y, 2, 2).wait_recv()

    group = 2 * conv * hl
    near_rows = []
    for j in range(3):
        near = buses[me + j].astype(jnp.float32) + float(sub * (j - 1) + 2 * REACH)
        near_rows += [near] * hl
    if 3 * group < LANES:
        near_rows.append(jnp.full((LANES - 3 * group, LANES), -1.0, jnp.float32))
    hit = jnp.concatenate(near_rows, axis=0).astype(jnp.int32) == lane
    part_one = lax.rem(tall, 8) < conv
    picks = [jnp.where(jnp.logical_and(hit, part_one), 1.0, 0.0)]
    picks.append(jnp.where(jnp.logical_and(hit, jnp.logical_not(part_one)), 1.0, 0.0))
    picks = jnp.concatenate(picks, axis=0).astype(jnp.bfloat16)
    taken = lax.dot_general(jnp.concatenate(rows_at, axis=0), picks, across, preferred_element_type=jnp.float32)
    harm_row = lax.rem(lax.broadcasted_iota(jnp.int32, full, 1), deep)
    same = harm_row == lax.rem(lane // 8, hl)
    answer = []
    for c in range(conv):
        cut = slice(flat[0] * c, flat[0] * (c + 1))
        whole = taken[cut, :LANES].reshape(full) + turned(taken[cut, LANES:].reshape(full))
        answer.append(jnp.where(same, whole, 0.0).astype(jnp.bfloat16))
    sorted_rows = []
    for b in range(nh // order):
        block_rows = [answer[c][order * b + i] for i in range(order) for c in range(conv)]
        mixed = jnp.dot(shuffle, jnp.concatenate(block_rows, axis=0), preferred_element_type=jnp.float32)
        sorted_rows.append(mixed.astype(jnp.bfloat16))

    row = lax.broadcasted_iota(jnp.int32, (rows, LANES), 0)
    is_real = row % 8 < conv
    base = jnp.bitwise_and((row // 8 - 1) * sub, 2 * LANES - 1)
    spread = []
    for t in range(tiles):
        near = buses[around * t : around * (t + 1) + 2].astype(jnp.float32).reshape(rows, LANES)
        at_bus = base + near.astype(jnp.int32)
        hits = [jnp.where(at_bus == lane + shift, 1.0, 0.0) for shift in (0, LANES)]
        spread.append(jnp.concatenate([hit.T for hit in hits], axis=0).astype(jnp.bfloat16))


    all_of(recv, nh - 1, 3, 3).wait_recv()

    @pl.when(has_left)
    def _():
        spec_copy(0, 0, y, 4, 4).wait_recv()

    @pl.when(has_right)
    def _():
        spec_copy(0, nh + 1, y, 5, 5).wait_recv()

    injected, solved, volts_now = [], [], []
    for t in range(tiles):
        parts = []
        for h in range(hl):
            here = recv[around * t : around * (t + 1) + 2, h].astype(jnp.float32).reshape(rows, LANES)
            parts += [jnp.where(is_real, here, 0.0), jnp.where(is_real, 0.0, here)]
        parts = jnp.concatenate(parts, axis=1).astype(jnp.bfloat16)
        injected.append(jnp.dot(spread[t], parts, preferred_element_type=jnp.float32).astype(jnp.bfloat16))
    for t in range(tiles):
        for h in range(hl):
            mine = injected[t][:, 2 * LANES * h : 2 * LANES * (h + 1)]
            solved.append(jnp.dot(resp[h, t], mine, preferred_element_type=jnp.float32))
    @pl.when(near_left)
    def _():
        near_copy(0, me, y).wait_recv()

    @pl.when(near_right)
    def _():
        near_copy(1, me, y).wait_recv()

    for t in range(tiles):
        now = []
        for h in range(hl):
            both = solved[t * hl + h]
            real = both[:LANES, :LANES] - both[LANES:, LANES:]
            imag = both[:LANES, LANES:] + both[LANES:, :LANES]
            now.append(jnp.concatenate([real, imag], axis=0).astype(jnp.bfloat16))
        volts_now.append(now)
    for t in range(tiles):
        for h in range(hl):
            out_ref[:, h, LANES * t : LANES * (t + 1)] = volts_now[t][h].reshape(2, LANES, LANES)

    for source in range(nh):
        around_here = jnp.concatenate(
            [near_spec[0, source].reshape(group, LANES), send[source].reshape(group, LANES)]
            + [near_spec[1, source].reshape(group, LANES)],
            axis=0,
        )
        at = size * (source % order)
        mine = sorted_rows[source // order][at : at + size, : 3 * group]
        at_conv = jnp.dot(mine, around_here, preferred_element_type=jnp.float32)
        at_conv = at_conv.reshape(2, deep, conv, LANES).astype(jnp.bfloat16)
        next_ref[:, hl * source : hl * (source + 1)] = at_conv[:, :hl]

    all_of(recv, nh - 1, 3, 3).wait_send()

    @pl.when(has_right)
    def _():
        for copy in side_copies(0):
            copy.wait_send()

    @pl.when(has_left)
    def _():
        for copy in side_copies(1):
            copy.wait_send()

    @pl.when(send_right)
    def _():
        all_of(buses, nh, 1, 1).wait_send()
        all_of(recv, nh, 4, 4).wait_send()

    @pl.when(send_left)
    def _():
        all_of(buses, nh, 2, 2).wait_send()
        all_of(recv, nh, 5, 5).wait_send()

    all_of(parcel_recv, nh - 1, 6, 6).wait_send()

    @pl.when(has_right)
    def _():
        edge_copy(0, me, y).wait_send()

    @pl.when(has_left)
    def _():
        edge_copy(1, me, y).wait_send()

    @pl.when(near_right)
    def _():
        near_copy(0, me, y).wait_send()

    @pl.when(near_left)
    def _():
        near_copy(1, me, y).wait_send()


def store(volt_ref, next_ref, volt_out, next_out, sems):
    copies = [pltpu.make_async_copy(volt_ref.at[p], volt_out.at[p], sems.at[p]) for p in range(2)]
    copies.append(pltpu.make_async_copy(next_ref, next_out, sems.at[2]))
    for copy in copies:
        copy.start()
    for copy in copies:
        copy.wait()


def local(nh, ny, conv_volt, conv_power, conv_type, type_steep, conv_bus, admittance, link_offset):
    _, orders, conv, snaps = conv_volt.shape
    hl = orders // nh
    block = admittance.shape[3]
    tiles = block // LANES
    around = LANES * nh // block
    deep = max(hl, 4)
    span = 2 * orders
    basis = make_basis(orders)
    regrouped = basis.reshape(2, orders, NT).transpose(1, 0, 2).reshape(span, NT)
    vmem = pl.BlockSpec(memory_space=pltpu.VMEM)
    anywhere = pl.BlockSpec(memory_space=pl.ANY)
    bf16 = jnp.bfloat16
    dma = pltpu.SemaphoreType.DMA
    volt_shape, next_shape = (2, hl, block, snaps), (2, orders, conv, snaps)
    solved = pl.pallas_call(
        functools.partial(kernel, nh, ny),
        out_shape=(pltpu.VMEM(volt_shape, bf16), pltpu.VMEM(next_shape, bf16)),
        in_specs=[anywhere] * 9,
        out_specs=(vmem, vmem),
        scratch_shapes=[
            pltpu.VMEM((span * conv, snaps), bf16),
            pltpu.SMEM(conv_type.shape, jnp.int32),
            pltpu.SMEM(type_steep.shape, jnp.float32),
            pltpu.VMEM((conv, snaps), jnp.float32),
            pltpu.SMEM(conv_bus.shape, jnp.int32),
            pltpu.VMEM(admittance.shape, jnp.float32),
            pltpu.VMEM(link_offset.shape, jnp.int32),
            pltpu.VMEM((NT, span), bf16),
            pltpu.VMEM((span, NT), bf16),
            pltpu.VMEM((span * conv + 8, LANES), jnp.float32),
            pltpu.VMEM((span, conv * LANES), bf16),
            pltpu.VMEM((nh, hl, 8, LANES), bf16),
            pltpu.VMEM((nh + 2, hl, 8, LANES), bf16),
            pltpu.VMEM((8, LANES), bf16),
            pltpu.VMEM((nh + 2, 8, LANES), bf16),
            pltpu.VMEM((2,) + admittance.shape[:3] + (LANES,), jnp.float32),
            pltpu.VMEM((2, link_offset.shape[0], LANES), jnp.int32),
            pltpu.VMEM((hl, tiles, 2 * LANES, 4 * LANES), bf16),
            pltpu.VMEM((hl, tiles, 2 * LANES, 2 * LANES), bf16),
            pltpu.VMEM((nh + 2, 3 * deep, LANES), bf16),
            pltpu.VMEM((nh, 3 * deep, LANES), bf16),
            pltpu.VMEM((nh, 3 * deep, LANES), bf16),
            pltpu.VMEM((2, nh, hl, 8, LANES), bf16),
            pltpu.VMEM((nh, 8, LANES), jnp.float32),
            dma((9,)),
            dma((15,)),
            dma((15,)),
        ],
        compiler_params=pltpu.CompilerParams(collective_id=0, has_side_effects=True, vmem_limit_bytes=56 * 2**20),
        name="power_flow",
    )(
        conv_volt.reshape(span * conv, snaps),
        conv_power,
        conv_type,
        type_steep,
        conv_bus,
        admittance,
        link_offset,
        jnp.asarray(basis.T, bf16),
        jnp.asarray(regrouped, bf16),
    )
    return pl.pallas_call(
        store,
        out_shape=(jax.ShapeDtypeStruct(volt_shape, bf16), jax.ShapeDtypeStruct(next_shape, bf16)),
        in_specs=[vmem, vmem],
        out_specs=(anywhere, anywhere),
        scratch_shapes=[dma((3,))],
        compiler_params=pltpu.CompilerParams(vmem_limit_bytes=32 * 2**20),
        name="store_results",
    )(*solved)


def solution(mesh):
    in_specs = (
        P(None, None, ("bus", "harm"), None),
        P(("bus", "harm"), None),
        P(("bus", "harm")),
        P(),
        P(("bus", "harm")),
        P(None, None, "harm", "bus"),
        P(None, "bus"),
    )
    out_specs = (P(None, "harm", "bus", None), P(None, None, ("bus", "harm"), None))
    body = functools.partial(local, mesh.shape["harm"], mesh.shape["bus"])
    return jax.shard_map(body, mesh=mesh, in_specs=in_specs, out_specs=out_specs, check_vma=False)
```
